128 devices in a mesh: expert: 8 (over z, core), ffn: 16 (over y, x).
Axes of the slice: x: 4, y: 4, z: 4, core: 2. Of those that a mesh axis runs over, the one named last changes fastest.
Arguments:
- tokens: bfloat16 [4096, 6144], P(('expert', 'ffn')), may hold values from -24 to 24
- expert_ids: int32 [4096, 2], P(('expert', 'ffn')), may hold values from 0 to 7, all different within a row; in each aligned block of 32 rows (0 to 31, 32 to 63, ...) at most 12 rows name the same one
- gate_weight: bfloat16 [8, 6144, 8192], P('expert', None, 'ffn'), may hold values from -0.078125 to 0.078125
- up_weight: bfloat16 [8, 6144, 8192], P('expert', None, 'ffn'), may hold values from -0.078125 to 0.078125
- down_weight: bfloat16 [8, 8192, 6144], P('expert', 'ffn'), may hold values from -0.0625 to 0.0625
- thresholds: float32 [8, 6144], P('expert'), may hold values from 0.002 to 0.01
Outputs:
- keep: bfloat16 [8, 8192, 6144], P('expert', 'ffn')
- kept_share: float32 [8, 6144], P('expert', 'ffn')
- input_rms: float32 [8, 6144], P('expert', 'ffn')
The draws below stay inside these ranges and needn't reach their ends.
Inputs may be any that keep to these rules, and one draw needn't show every extreme that they name: `expert_ids`: each row names two different experts. Among the 32 rows of one device no expert is named more than 12 times, and in some device some expert is named exactly 12 times.
All inputs are finite; a program needn't handle non-finite values.
Results may differ from the reference program's by a relative error of at most 0.001.
Values may be sent and summed in bfloat16 or wider, within the bound.
No kernel may reach another device: no remote copies, remote signals or barrier semaphores. Data moves between devices by JAX's collectives and lax.ppermute only.
A program may use at most 128 MiB of HBM per device.

```python
import math
import jax
import jax.numpy as jnp
import numpy as np
from jax import lax

D = 6144
FF = 8192
TOK_DEV = 32
E = 8
CAP = 12
TOKENS = 4096
N_EXPERT = 8
N_FFN = 16


def with_spikes(values, stream_key, source, target, shards_of, factor):
    def block_of(position):
        return (jnp.arange(values.shape[position]) // (values.shape[position] // shards_of)).reshape((-1,) + (1,) * (values.ndim - 1 - position))

    first = jax.random.permutation(stream_key, shards_of)[block_of(target)]
    far = (block_of(target) + shards_of // 2) % shards_of
    return jnp.where((block_of(source) == first) | (block_of(source) == far), factor * values, values)


def shard_levels(rng, extent, cuts, low, high):
    def one(position, shards_of):
        draws = jax.random.uniform(jax.random.fold_in(jax.random.fold_in(rng, 6), position), (shards_of,), jnp.float32, low / len(cuts), high / len(cuts))
        return jnp.repeat(jnp.exp(draws), extent[position] // shards_of).reshape((-1,) + (1,) * (len(extent) - position - 1))

    factor_of = one(*cuts[0])
    for cut in cuts[1:]:
        factor_of = factor_of * one(*cut)
    return factor_of


def assign_block(own_key, own, number, rows, count, top, bound, lean):
    ranking = jax.random.permutation(own_key, count)
    heavy_load, usual = shares(count, rows * top, bound, lean, True), shares(count, rows * top, bound, lean, False)
    places = jnp.arange(count)

    def named(sizes, turn):
        used = int((sizes > 0).sum())
        fixed = max(1, used // 4)
        moved = fixed + (places - fixed + turn * (used - fixed)) % max(1, count - fixed)
        return jnp.zeros((count,), jnp.int32).at[ranking[jnp.where(places < fixed, places, moved)]].set(jnp.asarray(sizes, jnp.int32))

    sizes = jnp.where(number % 4 == 0, named(heavy_load, number // 4), named(usual, number - number // 4 - 1))
    mixed = jax.random.permutation(jax.random.fold_in(own, 3), count)
    source_of, receiver = mixed[0:count // 2 * 2:2], mixed[1:count // 2 * 2:2]
    margin = jnp.minimum(sizes[source_of] - 1, bound - sizes[receiver]) // 2
    margin = jnp.where((source_of == ranking[0]) | (receiver == ranking[0]) | (sizes[receiver] == 0), 0, jnp.maximum(margin, 0))
    moved = jax.random.randint(jax.random.fold_in(own, 4), (count // 2,), 0, 1 << 20) % (margin + 1)
    sizes = sizes.at[source_of].add(-moved).at[receiver].add(moved)
    items = jnp.searchsorted(jnp.cumsum(sizes), jnp.arange(rows * top), side="right").astype(jnp.int32)
    listing = items.reshape(top, rows).T
    listing = listing[jax.random.permutation(jax.random.fold_in(own, 1), rows)]
    turn = jax.random.randint(jax.random.fold_in(own, 2), (rows, 1), 0, top)
    return jnp.take_along_axis(listing, (jnp.arange(top)[None, :] + turn) % top, axis=1)


def shares(count, total, most, skew, full):
    portions = [(1 << 20) // math.isqrt(standing ** skew) + 1 for standing in range(1, count + 1)]
    largest = most if full else min(most, max(-(-total // count), total * portions[0] // sum(portions)))
    least = 1 if total - largest >= count - 1 else 0
    holding, rest = [largest] + [least] * (count - 1), total - largest - least * (count - 1)
    while rest > 0:
        movable = [i for i in range(1, count) if holding[i] < largest] or [i for i in range(1, count) if holding[i] < most]
        whole, remaining = sum([portions[i] for i in movable]), rest
        for i in movable:
            more = min(most - holding[i], max(1, remaining * portions[i] // whole), rest)
            holding[i] = holding[i] + more
            rest = rest - more
    return np.array(holding)


def scatter_about(key, extent, scale, reach, pieces=(), kind=jnp.bfloat16):
    level = shard_levels(key, extent, pieces, -0.22, 0.18) if pieces else 1.0
    drawn = jax.random.normal(key, extent, jnp.float32) * scale * level
    return jnp.minimum(jnp.maximum(drawn, -reach), reach).astype(kind)


def noise_with(stream_key, shape, scale, reach, shards, heavy, held_as=jnp.bfloat16):
    values = scale * jax.random.normal(stream_key, shape, jnp.float32)
    if shards:
        values = values * shard_levels(stream_key, shape, shards, -0.22, 0.18)
    return jnp.clip(with_spikes(values, jax.random.fold_in(stream_key, 3), *heavy), -reach, reach).astype(held_as)


def setup_inputs(seed: int = 0) -> dict:
    key_list = jax.random.split(jax.random.key(seed), 7)
    tokens = noise_with(key_list[0], (TOKENS, D), 1.0, 24.0, ((0, 128),), (0, 1, 128, 5.5))
    expert_ids_keys = jax.random.split(jax.random.fold_in(key_list[1], 1), TOKENS // TOK_DEV)
    expert_ids_turns = jax.random.permutation(jax.random.fold_in(key_list[1], 3), TOKENS // TOK_DEV)
    expert_ids = jax.vmap(lambda own, number: assign_block(jax.random.fold_in(key_list[1], 2), own, number, TOK_DEV, E, 2, CAP, 2))(expert_ids_keys, expert_ids_turns).reshape((TOKENS, 2))
    gate_weight = scatter_about(key_list[2], (E, D, FF), D ** -0.5, 0.078125, ((0, 8), (2, 16)))
    up_weight = scatter_about(key_list[3], (E, D, FF), D ** -0.5, 0.078125, ((0, 8), (2, 16)))
    down_weight = scatter_about(key_list[4], (E, FF, D), FF ** -0.5, 0.0625, ((0, 8), (1, 16)))
    thresholds = jnp.clip(jnp.exp(math.log(0.01) - 1.6094378 * jax.random.uniform(key_list[5], (E, D), jnp.float32) ** shard_levels(key_list[5], (E, D), ((0, 8),), -0.2, 0.2)), 0.002, 0.01)
    return dict(tokens=tokens, expert_ids=expert_ids, gate_weight=gate_weight, up_weight=up_weight, down_weight=down_weight, thresholds=thresholds)


def reference(tokens, expert_ids, gate_weight, up_weight, down_weight, thresholds):
    slots = N_EXPERT * N_FFN * CAP

    def one_expert(expert):
        routed = jnp.any(expert_ids == expert, axis=1)
        count = jnp.sum(routed.astype(jnp.float32))
        index = jnp.nonzero(routed, size=slots, fill_value=0)[0].astype(jnp.int32)
        live = jnp.arange(slots, dtype=jnp.int32) < jnp.sum(routed.astype(jnp.int32))
        rows = jnp.where(live[:, None], jnp.take(tokens, index, axis=0), jnp.zeros((), tokens.dtype))
        gate = jnp.dot(rows, gate_weight[expert], preferred_element_type=jnp.float32)
        up = jnp.dot(rows, up_weight[expert], preferred_element_type=jnp.float32)
        hidden = jax.nn.silu(gate) * up
        hidden_rms = jnp.sqrt(lax.optimization_barrier(jnp.sum(hidden * hidden, axis=0)) / count)
        squares = jnp.where(routed[:, None], jnp.square(tokens.astype(jnp.float32)), jnp.zeros((), jnp.float32))
        input_rms = jnp.sqrt(lax.optimization_barrier(jnp.sum(squares, axis=0)) / count)
        score = jnp.abs(down_weight[expert].astype(jnp.float32)) * hidden_rms[:, None]
        keep = jnp.clip(16.0 * (score / thresholds[expert][None, :] - 1.0) + 0.5, 0.0, 1.0)
        share = lax.optimization_barrier(jnp.sum(keep, axis=0)) / FF
        return (keep.astype(jnp.bfloat16), share, input_rms)
    keep, share, input_rms = lax.map(one_expert, jnp.arange(E, dtype=jnp.int32))
    return (keep, share, input_rms)
```

```python
import jax
import jax.numpy as jnp
from jax import lax
from jax.experimental import pallas as pl
from jax.experimental.pallas import tpu as pltpu
from jax.sharding import PartitionSpec as P

FF = 8192
CAP = 12
MARK = 512.0
LIMIT = 100.0
RING = 4
AXES = ("expert", "ffn")
STEP = 768
KEEP_COLS = 768
MIB = 1 << 20


def moved(value, core0, core1):
    pairs = []
    for z in range(RING):
        for c in range(2):
            for y in range(RING):
                for x in range(RING):
                    dz, dc, dy, dx = core1 if c else core0
                    src = ((z * 2 + c) * RING + y) * RING + x
                    to = (((z + dz) % RING) * 2 + (c + dc) % 2) * RING + (y + dy) % RING
                    pairs.append((src, to * RING + (x + dx) % RING))
    return lax.ppermute(value, AXES, pairs)


def over_z(value, step):
    return moved(value, (step, 0, 0, 0), (step, 0, 0, 0))


def to_other_core(value):
    return moved(value, (0, 1, 0, 0), (0, 1, 0, 0))


def first_way(value, step):
    return moved(value, (0, 0, 0, step), (0, 0, step, 0))


def second_way(value, step):
    return moved(value, (0, 0, step, 0), (0, 0, 0, step))


def pack_kernel(ids_ref, tokens_ref, near_ref, near_send_ref, far_ref, far_send_ref):
    expert = lax.axis_index("expert")
    z, c = expert // 2, expert % 2
    rows = tokens_ref[...]
    count = rows.shape[0]
    ids = ids_ref[...]
    before = lax.broadcasted_iota(jnp.int32, (count, count), 0) < lax.broadcasted_iota(
        jnp.int32, (count, count), 1
    )
    before = before.astype(jnp.float32).astype(jnp.bfloat16)

    def packed(out_ref, core, shifts):
        size = 2 * CAP * len(shifts)
        row = lax.broadcasted_iota(jnp.int32, (size, count), 0)
        group = row // (2 * CAP)
        slot = row - group * (2 * CAP) - c * CAP
        mine = (slot >= 0) & (slot < CAP)
        wanted = jnp.zeros((size, count), jnp.int32)
        for i, shift in enumerate(shifts):
            wanted = jnp.where(group == i, ((z + shift) % RING) * 2 + core, wanted)
        routed = (ids[0:1, :] == wanted) | (ids[1:2, :] == wanted)
        mark = routed.astype(jnp.float32)
        rank = jnp.dot(mark.astype(jnp.bfloat16), before, preferred_element_type=jnp.float32)
        pick = jnp.where(routed & mine & (rank.astype(jnp.int32) == slot), 1.0, 0.0)
        filled = jnp.sum(pick, axis=1, keepdims=True)
        out = jnp.dot(pick.astype(jnp.bfloat16), rows, preferred_element_type=jnp.float32)
        out_ref[...] = out.astype(jnp.bfloat16)
        head = out[:, :128]
        lane = lax.broadcasted_iota(jnp.int32, head.shape, 1)
        empty = (lane == 0) & (filled < 0.5) & mine[:, 0:1]
        out_ref[:, :128] = jnp.where(empty, MARK, head).astype(jnp.bfloat16)

    packed(near_ref, c, (0,))
    packed(near_send_ref, 1 - c, (0,))
    packed(far_ref, c, (1, 2, 3))
    packed(far_send_ref, 1 - c, (1, 2, 3))


def pack(tokens, expert_ids):
    width = tokens.shape[1]
    sizes = (2 * CAP, 2 * CAP, 6 * CAP, 6 * CAP)
    return pl.pallas_call(
        pack_kernel,
        out_shape=[jax.ShapeDtypeStruct((n, width), tokens.dtype) for n in sizes],
        compiler_params=pltpu.CompilerParams(vmem_limit_bytes=24 * MIB),
        name="pack_rows",
    )(expert_ids.T, tokens)


def join_kernel(*refs):
    xs, (out_ref, sem) = refs[:-2], refs[-2:]
    copies, at = [], 0
    for i, x_ref in enumerate(xs):
        n = x_ref.shape[0]
        copies.append(pltpu.make_async_copy(x_ref, out_ref.at[pl.ds(at, n)], sem.at[i]))
        at += n
    for copy in copies:
        copy.start()
    for copy in copies:
        copy.wait()


def joined(*xs):
    return pl.pallas_call(
        join_kernel,
        in_specs=[pl.BlockSpec(memory_space=pl.ANY)] * len(xs),
        out_specs=pl.BlockSpec(memory_space=pltpu.VMEM),
        out_shape=jax.ShapeDtypeStruct((sum(x.shape[0] for x in xs), xs[0].shape[1]), xs[0].dtype),
        scratch_shapes=[pltpu.SemaphoreType.DMA((len(xs),))],
        compiler_params=pltpu.CompilerParams(vmem_limit_bytes=24 * MIB),
        name="join_rows",
    )(*xs)


def after(value, *others):
    return lax.optimization_barrier((value, *others))[0]


def stats_kernel(n, *refs):
    xs, (gate_ref, up_ref, hid_in, feat_in, hid_ref, feat_ref, g_acc, u_acc) = refs[:n], refs[n:]
    k = pl.program_id(0)
    f = lax.axis_index("ffn")

    def rows_of(cols):
        parts = [x_ref[:, cols] for x_ref in xs]
        return parts[0] if n == 1 else jnp.concatenate(parts, axis=0)

    @pl.when(k == 0)
    def _():
        x = rows_of(slice(None))
        x = jnp.where(x > LIMIT, jnp.zeros_like(x), x)
        g_acc[...] = jnp.dot(x, gate_ref[...], preferred_element_type=jnp.float32)
        u_acc[...] = jnp.dot(x, up_ref[...], preferred_element_type=jnp.float32)
        live = jnp.where(rows_of(slice(0, 128)).astype(jnp.float32) > LIMIT, 0.0, 1.0)
        feat_ref[:, 384:] = feat_in[:, 384:] + jnp.sum(live, axis=0, keepdims=True)
        feat_ref[:, :384] = feat_in[:, :384]

    @pl.when(k > 0)
    def _():
        x = rows_of(slice(None))
        g_acc[...] += jnp.dot(x, gate_ref[...], preferred_element_type=jnp.float32)
        u_acc[...] += jnp.dot(x, up_ref[...], preferred_element_type=jnp.float32)

    @pl.when(k == f // 2)
    def _():
        part = rows_of(pl.ds(pl.multiple_of((f % 2) * 384, 128), 384)).astype(jnp.float32)
        part = jnp.where(part > LIMIT, 0.0, part)
        feat_ref[:, :384] += jnp.sum(part * part, axis=0, keepdims=True)

    @pl.when(k == pl.num_programs(0) - 1)
    def _():
        g = g_acc[...]
        h = g / (1.0 + jnp.exp(-g)) * u_acc[...]
        hid_ref[...] = hid_in[...] + jnp.sum(h * h, axis=0, keepdims=True)


def add_stats(xs, gate, up, hid, feat):
    width, units = gate.shape
    rows = sum(x.shape[0] for x in xs)
    return pl.pallas_call(
        lambda *refs: stats_kernel(len(xs), *refs),
        grid=(width // STEP,),
        in_specs=[pl.BlockSpec((x.shape[0], STEP), lambda k: (0, k)) for x in xs]
        + [pl.BlockSpec((STEP, units), lambda k: (k, 0))] * 2
        + [pl.BlockSpec(hid.shape, lambda k: (0, 0)), pl.BlockSpec(feat.shape, lambda k: (0, 0))],
        out_specs=[
            pl.BlockSpec(hid.shape, lambda k: (0, 0)),
            pl.BlockSpec(feat.shape, lambda k: (0, 0)),
        ],
        out_shape=[
            jax.ShapeDtypeStruct(hid.shape, jnp.float32),
            jax.ShapeDtypeStruct(feat.shape, jnp.float32),
        ],
        scratch_shapes=[pltpu.VMEM((rows, units), jnp.float32)] * 2,
        cost_estimate=pl.CostEstimate(
            flops=4 * rows * width * units,
            transcendentals=rows * units,
            bytes_accessed=2 * width * (rows + 2 * units),
        ),
        compiler_params=pltpu.CompilerParams(vmem_limit_bytes=32 * MIB),
        name="hidden_stats",
    )(*xs, gate, up, hid, feat)


def keep_kernel(hid_ref, feat_ref, down_ref, thr_ref, keep_ref, share_ref, scale_ref):
    @pl.when(pl.program_id(0) == 0)
    def _():
        rms = jnp.sqrt(hid_ref[...] / feat_ref[:, 384:385])
        wide = jnp.broadcast_to(16.0 * rms, (8, rms.shape[1]))
        scale_ref[...] = wide.T

    inverse = 1.0 / thr_ref[...]
    score = jnp.abs(down_ref[...].astype(jnp.float32)) * scale_ref[:, 0:1]
    keep = jnp.clip(score * inverse - 15.5, 0.0, 1.0)
    keep_ref[...] = keep.astype(keep_ref.dtype)
    share_ref[...] = jnp.sum(keep, axis=0, keepdims=True) * (1.0 / FF)


def keep_pass(hid, feat, down, thresholds):
    units, width = down.shape
    return pl.pallas_call(
        keep_kernel,
        grid=(width // KEEP_COLS,),
        in_specs=[
            pl.BlockSpec(hid.shape, lambda j: (0, 0)),
            pl.BlockSpec(feat.shape, lambda j: (0, 0)),
            pl.BlockSpec((units, KEEP_COLS), lambda j: (0, j)),
            pl.BlockSpec((1, KEEP_COLS), lambda j: (0, j)),
        ],
        out_specs=[
            pl.BlockSpec((units, KEEP_COLS), lambda j: (0, j)),
            pl.BlockSpec((1, KEEP_COLS), lambda j: (0, j)),
        ],
        out_shape=[
            jax.ShapeDtypeStruct((units, width), down.dtype),
            jax.ShapeDtypeStruct((1, width), jnp.float32),
        ],
        scratch_shapes=[pltpu.VMEM((units, 8), jnp.float32)],
        compiler_params=pltpu.CompilerParams(vmem_limit_bytes=32 * MIB),
        name="keep_pass",
    )(hid, feat, down, thresholds)


def per_device(tokens, expert_ids, gate_weight, up_weight, down_weight, thresholds):
    gate, up = gate_weight[0], up_weight[0]
    near, near_send, far, far_send = pack(tokens, expert_ids)
    own = near + to_other_core(near_send)
    far = far + to_other_core(far_send)
    ahead, behind = over_z(far[:40], 1), over_z(far[40:], -1)
    left, right = first_way(own, 1), first_way(own, -1)

    tied = lax.optimization_barrier((ahead[24:], behind[:8], left, right))
    across = over_z(tied[0], 1), over_z(tied[1], -1)
    left, right = tied[2:]
    corner = first_way(left[:16], 1), first_way(right[16:], -1)
    own_line = joined(own, left, right, *corner)

    rest = after(joined(ahead[:24], behind[8:], *across), own_line)
    near_sides = second_way(own_line, 1), second_way(own_line, -1)
    left, right = first_way(rest, 1), first_way(rest, -1)
    corner = first_way(left[:40], 1), first_way(right[40:], -1)
    near_corner = second_way(near_sides[0][:48], 1), second_way(near_sides[1][48:], -1)
    rest_line = after(joined(rest, left, right, *corner), *near_corner)
    sides = second_way(rest_line, 1), second_way(rest_line, -1)

    hid = jnp.zeros((1, 512), jnp.float32)
    feat = jnp.zeros((1, 512), jnp.float32)
    hid, feat = add_stats([own_line, *near_sides, *near_corner], gate, up, hid, feat)
    hid, feat = add_stats([rest_line], gate, up, hid, feat)
    tied = lax.optimization_barrier((sides, hid, feat))
    sides, hid, feat = tied
    far_corner = second_way(sides[0][:144], 1), second_way(sides[1][144:], -1)
    hid, feat = add_stats(list(sides), gate, up, hid, feat)
    hid, feat = add_stats(list(far_corner), gate, up, hid, feat)
    input_rms = jnp.sqrt(feat[:, :384] / feat[:, 384:385])
    keep, share = keep_pass(hid, feat, down_weight[0], thresholds)
    pieces = lax.all_to_all(share.reshape(16, 1, 384), "ffn", 0, 0, tiled=True)
    return keep[None], jnp.sum(pieces, axis=0), input_rms


def solution(mesh):
    in_specs = (
        P(("expert", "ffn"), None),
        P(("expert", "ffn"), None),
        P("expert", None, "ffn"),
        P("expert", None, "ffn"),
        P("expert", "ffn", None),
        P("expert", None),
    )
    out_specs = (P("expert", "ffn", None), P("expert", "ffn"), P("expert", "ffn"))
    return jax.shard_map(
        per_device, mesh=mesh, in_specs=in_specs, out_specs=out_specs, check_vma=False
    )
```

```python
import jax
import jax.numpy as jnp
from jax import lax
from jax.experimental import pallas as pl
from jax.experimental.pallas import tpu as pltpu
from jax.sharding import PartitionSpec as P

FF = 8192
CAP = 12
MARK = 512.0
LIMIT = 100.0
RING = 4
AXES = ("expert", "ffn")
STEP = 768
KEEP_COLS = 768
SHARE_COLS = 256
MIB = 1 << 20


def moved(value, core0, core1):
    pairs = []
    for z in range(RING):
        for c in range(2):
            for y in range(RING):
                for x in range(RING):
                    dz, dc, dy, dx = core1 if c else core0
                    src = ((z * 2 + c) * RING + y) * RING + x
                    to = (((z + dz) % RING) * 2 + (c + dc) % 2) * RING + (y + dy) % RING
                    pairs.append((src, to * RING + (x + dx) % RING))
    return lax.ppermute(value, AXES, pairs)


def over_z(value, step):
    return moved(value, (step, 0, 0, 0), (step, 0, 0, 0))


def to_other_core(value):
    return moved(value, (0, 1, 0, 0), (0, 1, 0, 0))


def first_way(value, step):
    return moved(value, (0, 0, 0, step), (0, 0, step, 0))


def second_way(value, step):
    return moved(value, (0, 0, step, 0), (0, 0, 0, step))


def pack_kernel(ids_ref, tokens_ref, near_ref, near_send_ref, far_ref, far_send_ref):
    expert = lax.axis_index("expert")
    z, c = expert // 2, expert % 2
    rows = tokens_ref[...]
    count = rows.shape[0]
    ids = ids_ref[...]
    before = lax.broadcasted_iota(jnp.int32, (count, count), 0) < lax.broadcasted_iota(
        jnp.int32, (count, count), 1
    )
    before = before.astype(jnp.float32).astype(jnp.bfloat16)

    def packed(out_ref, core, shifts):
        size = 2 * CAP * len(shifts)
        row = lax.broadcasted_iota(jnp.int32, (size, count), 0)
        group = row // (2 * CAP)
        slot = row - group * (2 * CAP) - c * CAP
        mine = (slot >= 0) & (slot < CAP)
        wanted = jnp.zeros((size, count), jnp.int32)
        for i, shift in enumerate(shifts):
            wanted = jnp.where(group == i, ((z + shift) % RING) * 2 + core, wanted)
        routed = (ids[0:1, :] == wanted) | (ids[1:2, :] == wanted)
        mark = routed.astype(jnp.float32)
        rank = jnp.dot(mark.astype(jnp.bfloat16), before, preferred_element_type=jnp.float32)
        pick = jnp.where(routed & mine & (rank.astype(jnp.int32) == slot), 1.0, 0.0)
        filled = jnp.sum(pick, axis=1, keepdims=True)
        out = jnp.dot(pick.astype(jnp.bfloat16), rows, preferred_element_type=jnp.float32)
        out_ref[...] = out.astype(jnp.bfloat16)
        head = out[:, :128]
        lane = lax.broadcasted_iota(jnp.int32, head.shape, 1)
        empty = (lane == 0) & (filled < 0.5) & mine[:, 0:1]
        out_ref[:, :128] = jnp.where(empty, MARK, head).astype(jnp.bfloat16)

    packed(near_ref, c, (0,))
    packed(near_send_ref, 1 - c, (0,))
    packed(far_ref, c, (1, 2, 3))
    packed(far_send_ref, 1 - c, (1, 2, 3))


def pack(tokens, expert_ids):
    width = tokens.shape[1]
    sizes = (2 * CAP, 2 * CAP, 6 * CAP, 6 * CAP)
    return pl.pallas_call(
        pack_kernel,
        out_shape=[jax.ShapeDtypeStruct((n, width), tokens.dtype) for n in sizes],
        compiler_params=pltpu.CompilerParams(vmem_limit_bytes=12 * MIB),
        name="pack_rows",
    )(expert_ids.T, tokens)


def join_kernel(n, *refs):
    xs, outs, sem = refs[:n], refs[n:-1], refs[-1]
    copies, at = [], 0
    for i, x_ref in enumerate(xs):
        out_ref = outs[at // outs[0].shape[0]]
        rows = pl.ds(at % outs[0].shape[0], x_ref.shape[0])
        copies.append(pltpu.make_async_copy(x_ref, out_ref.at[rows], sem.at[i]))
        at += x_ref.shape[0]
    for copy in copies:
        copy.start()
    for copy in copies:
        copy.wait()


def joined(xs, parts):
    rows = sum(x.shape[0] for x in xs) // parts
    return pl.pallas_call(
        lambda *refs: join_kernel(len(xs), *refs),
        in_specs=[pl.BlockSpec(memory_space=pl.ANY)] * len(xs),
        out_specs=[pl.BlockSpec(memory_space=pltpu.VMEM)] * parts,
        out_shape=[jax.ShapeDtypeStruct((rows, xs[0].shape[1]), xs[0].dtype)] * parts,
        scratch_shapes=[pltpu.SemaphoreType.DMA((len(xs),))],
        compiler_params=pltpu.CompilerParams(vmem_limit_bytes=12 * MIB),
        name="join_rows",
    )(*xs)


def after(value, *others):
    return lax.optimization_barrier((value, *others))[0]


def stats_kernel(n, *refs):
    xs, (gate_ref, up_ref, hid_in, feat_in, hid_ref, feat_ref, g_acc, u_acc) = refs[:n], refs[n:]
    f = lax.axis_index("ffn")

    def rows_of(cols):
        parts = [x_ref[:, cols] for x_ref in xs]
        return parts[0] if n == 1 else jnp.concatenate(parts, axis=0)

    x = rows_of(slice(0, STEP))
    x = jnp.where(x > LIMIT, jnp.zeros_like(x), x)
    g_acc[...] = jnp.dot(x, gate_ref[:STEP, :], preferred_element_type=jnp.float32)
    u_acc[...] = jnp.dot(x, up_ref[:STEP, :], preferred_element_type=jnp.float32)

    def step(k, carry):
        cols = pl.ds(pl.multiple_of(k * STEP, STEP), STEP)
        x = rows_of(cols)
        g_acc[...] += jnp.dot(x, gate_ref[cols, :], preferred_element_type=jnp.float32)
        u_acc[...] += jnp.dot(x, up_ref[cols, :], preferred_element_type=jnp.float32)
        return carry

    lax.fori_loop(1, gate_ref.shape[0] // STEP, step, 0)
    live = jnp.where(rows_of(slice(0, 128)).astype(jnp.float32) > LIMIT, 0.0, 1.0)
    feat_ref[:, 384:] = feat_in[:, 384:] + jnp.sum(live, axis=0, keepdims=True)
    part = rows_of(pl.ds(pl.multiple_of(f * 384, 128), 384)).astype(jnp.float32)
    part = jnp.where(part > LIMIT, 0.0, part)
    feat_ref[:, :384] = feat_in[:, :384] + jnp.sum(part * part, axis=0, keepdims=True)
    g = g_acc[...]
    h = g / (1.0 + jnp.exp(-g)) * u_acc[...]
    hid_ref[...] = hid_in[...] + jnp.sum(h * h, axis=0, keepdims=True)


def add_stats(xs, gate, up, hid, feat):
    width, units = gate.shape
    rows = sum(x.shape[0] for x in xs)
    vmem = pl.BlockSpec(memory_space=pltpu.VMEM)
    return pl.pallas_call(
        lambda *refs: stats_kernel(len(xs), *refs),
        in_specs=[vmem] * (len(xs) + 4),
        out_specs=[vmem] * 2,
        out_shape=[
            jax.ShapeDtypeStruct(hid.shape, jnp.float32),
            jax.ShapeDtypeStruct(feat.shape, jnp.float32),
        ],
        scratch_shapes=[pltpu.VMEM((rows, units), jnp.float32)] * 2,
        cost_estimate=pl.CostEstimate(
            flops=4 * rows * width * units,
            transcendentals=rows * units,
            bytes_accessed=2 * width * rows,
        ),
        compiler_params=pltpu.CompilerParams(vmem_limit_bytes=16 * MIB),
        name="hidden_stats",
    )(*xs, gate, up, hid, feat)


def scale_of(hid_ref, feat_ref):
    rms = jnp.sqrt(hid_ref[...] / feat_ref[:, 384:385])
    return jnp.broadcast_to(16.0 * rms, (8, rms.shape[1])).T


def keep_of(down, scale, thresholds):
    score = jnp.abs(down.astype(jnp.float32)) * scale
    return jnp.clip(score * (1.0 / thresholds) - 15.5, 0.0, 1.0)


def share_kernel(hid_ref, feat_ref, down_ref, thr_ref, share_ref, scale_ref):
    scale_ref[...] = scale_of(hid_ref, feat_ref)

    def block(j, carry):
        cols = pl.ds(pl.multiple_of(j * SHARE_COLS, SHARE_COLS), SHARE_COLS)
        thresholds = thr_ref[:, cols]
        total = jnp.zeros((8, SHARE_COLS), jnp.float32)
        for u in range(0, down_ref.shape[0], 64):
            keep = keep_of(down_ref[u : u + 64, cols], scale_ref[u : u + 64, 0:1], thresholds)
            total += jnp.sum(keep.reshape(8, 8, SHARE_COLS), axis=0)
        share_ref[:, cols] = jnp.sum(total, axis=0, keepdims=True) * (1.0 / FF)
        return carry

    lax.fori_loop(0, down_ref.shape[1] // SHARE_COLS, block, 0)


def share_pass(hid, feat, down, thresholds):
    vmem = pl.BlockSpec(memory_space=pltpu.VMEM)
    return pl.pallas_call(
        share_kernel,
        in_specs=[vmem] * 4,
        out_specs=vmem,
        out_shape=jax.ShapeDtypeStruct((1, down.shape[1]), jnp.float32),
        scratch_shapes=[pltpu.VMEM((down.shape[0], 8), jnp.float32)],
        compiler_params=pltpu.CompilerParams(vmem_limit_bytes=8 * MIB),
        name="share_pass",
    )(hid, feat, down, thresholds)


def keep_kernel(hid_ref, feat_ref, down_ref, thr_ref, keep_ref, scale_ref):
    @pl.when(pl.program_id(0) == 0)
    def _():
        scale_ref[...] = scale_of(hid_ref, feat_ref)

    keep_ref[...] = keep_of(down_ref[...], scale_ref[:, 0:1], thr_ref[...]).astype(keep_ref.dtype)


def keep_pass(hid, feat, down, thresholds):
    units, width = down.shape
    return pl.pallas_call(
        keep_kernel,
        grid=(width // KEEP_COLS,),
        in_specs=[
            pl.BlockSpec(hid.shape, lambda j: (0, 0)),
            pl.BlockSpec(feat.shape, lambda j: (0, 0)),
            pl.BlockSpec((units, KEEP_COLS), lambda j: (0, j)),
            pl.BlockSpec((1, KEEP_COLS), lambda j: (0, j)),
        ],
        out_specs=pl.BlockSpec((units, KEEP_COLS), lambda j: (0, j)),
        out_shape=jax.ShapeDtypeStruct((units, width), down.dtype),
        scratch_shapes=[pltpu.VMEM((units, 8), jnp.float32)],
        compiler_params=pltpu.CompilerParams(vmem_limit_bytes=12 * MIB),
        name="keep_pass",
    )(hid, feat, down, thresholds)


def per_device(tokens, expert_ids, gate_weight, up_weight, down_weight, thresholds):
    gate, up, down = gate_weight[0], up_weight[0], down_weight[0]
    near, near_send, far, far_send = pack(tokens, expert_ids)
    own = near + to_other_core(near_send)
    far = far + to_other_core(far_send)
    ahead, behind = over_z(far[:40], 1), over_z(far[40:], -1)
    left, right = first_way(own, 1), first_way(own, -1)
    corner = first_way(left[:16], 1), first_way(right[16:], -1)
    [own_line] = joined([own, left, right, *corner], 1)

    ahead, behind, own_line = lax.optimization_barrier((ahead, behind, own_line))
    near_sides = second_way(own_line, 1), second_way(own_line, -1)
    across = over_z(ahead[24:], 1), over_z(behind[:8], -1)
    [rest] = joined([ahead[:24], behind[8:], *across], 1)
    left, right = first_way(rest, 1), first_way(rest, -1)
    corner = first_way(left[:40], 1), first_way(right[40:], -1)
    near_corner = second_way(near_sides[0][:48], 1), second_way(near_sides[1][48:], -1)

    corner, near_corner = lax.optimization_barrier((corner, near_corner))
    head, tail = joined([rest, left, right, *corner], 2)
    left, right = second_way(head, 1), second_way(tail, -1)
    left_too, right_too = second_way(tail, 1), second_way(head, -1)

    hid = jnp.zeros((1, 512), jnp.float32)
    feat = jnp.zeros((1, 512), jnp.float32)
    hid, feat = add_stats([own_line, *near_sides, *near_corner], gate, up, hid, feat)
    far_corner = second_way(left, 1), second_way(right, -1)
    hid, feat = add_stats([head, tail], gate, up, hid, feat)
    hid, feat = add_stats([left, right], gate, up, hid, feat)
    hid, feat = add_stats([left_too, right_too], gate, up, hid, feat)
    hid, feat = add_stats(list(far_corner), gate, up, hid, feat)
    input_rms = jnp.sqrt(feat[:, :384] / feat[:, 384:385])
    share = share_pass(hid, feat, down, thresholds)
    pieces = lax.all_to_all(share.reshape(16, 1, 384), "ffn", 0, 0, tiled=True)
    keep = keep_pass(hid, feat, down, thresholds)
    return keep[None], jnp.sum(pieces, axis=0), input_rms


def solution(mesh):
    in_specs = (
        P(("expert", "ffn"), None),
        P(("expert", "ffn"), None),
        P("expert", None, "ffn"),
        P("expert", None, "ffn"),
        P("expert", "ffn", None),
        P("expert", None),
    )
    out_specs = (P("expert", "ffn", None), P("expert", "ffn"), P("expert", "ffn"))
    return jax.shard_map(
        per_device, mesh=mesh, in_specs=in_specs, out_specs=out_specs, check_vma=False
    )
```

```python
import jax
import jax.numpy as jnp
from jax import lax
from jax.experimental import pallas as pl
from jax.experimental.pallas import tpu as pltpu
from jax.sharding import PartitionSpec as P

FF = 8192
CAP = 12
MARK = 512.0
LIMIT = 100.0
RING = 4
AXES = ("expert", "ffn")
STEP = 768
KEEP_ROWS = 64
KEEP_COLS = 512
SHARE_COLS = 256
MIB = 1 << 20
SMALL = pl.CostEstimate(flops=0, transcendentals=0, bytes_accessed=0)


def moved(value, core0, core1):
    pairs = []
    for z in range(RING):
        for c in range(2):
            for y in range(RING):
                for x in range(RING):
                    dz, dc, dy, dx = core1 if c else core0
                    src = ((z * 2 + c) * RING + y) * RING + x
                    to = (((z + dz) % RING) * 2 + (c + dc) % 2) * RING + (y + dy) % RING
                    pairs.append((src, to * RING + (x + dx) % RING))
    return lax.ppermute(value, AXES, pairs)


def over_z(value, step):
    return moved(value, (step, 0, 0, 0), (step, 0, 0, 0))


def to_other_core(value):
    return moved(value, (0, 1, 0, 0), (0, 1, 0, 0))


def first_way(value, step):
    return moved(value, (0, 0, 0, step), (0, 0, step, 0))


def second_way(value, step):
    return moved(value, (0, 0, step, 0), (0, 0, 0, step))


def pack_kernel(ids_ref, tokens_ref, near_ref, far_ref):
    expert = lax.axis_index("expert")
    z, c = expert // 2, expert % 2
    rows = tokens_ref[...]
    count = rows.shape[0]
    ids = ids_ref[...]
    before = lax.broadcasted_iota(jnp.int32, (count, count), 0) < lax.broadcasted_iota(
        jnp.int32, (count, count), 1
    )
    before = before.astype(jnp.float32).astype(jnp.bfloat16)

    def packed(out_ref, shifts):
        size = 2 * CAP * len(shifts)
        row = lax.broadcasted_iota(jnp.int32, (size, count), 0)
        group = row // CAP
        slot = row - group * CAP
        wanted = jnp.zeros((size, count), jnp.int32)
        for i, shift in enumerate(shifts):
            for j, core in enumerate((c, 1 - c)):
                chip = (z + shift) % RING
                wanted = jnp.where(group == 2 * i + j, chip * 2 + core, wanted)
        routed = (ids[0:1, :] == wanted) | (ids[1:2, :] == wanted)
        mark = routed.astype(jnp.float32)
        rank = jnp.dot(mark.astype(jnp.bfloat16), before, preferred_element_type=jnp.float32)
        pick = jnp.where(routed & (rank.astype(jnp.int32) == slot), 1.0, 0.0)
        filled = jnp.sum(pick, axis=1, keepdims=True)
        out = jnp.dot(pick.astype(jnp.bfloat16), rows, preferred_element_type=jnp.float32)
        out_ref[...] = out.astype(jnp.bfloat16)
        head = out[:, :128]
        lane = lax.broadcasted_iota(jnp.int32, head.shape, 1)
        empty = (lane == 0) & (filled < 0.5)
        out_ref[:, :128] = jnp.where(empty, MARK, head).astype(jnp.bfloat16)

    packed(near_ref, (0,))
    packed(far_ref, (1, 2, 3))


def pack(tokens, expert_ids):
    width = tokens.shape[1]
    return pl.pallas_call(
        pack_kernel,
        out_shape=[jax.ShapeDtypeStruct((n * CAP, width), tokens.dtype) for n in (2, 6)],
        compiler_params=pltpu.CompilerParams(vmem_limit_bytes=12 * MIB),
        cost_estimate=SMALL,
        name="pack_rows",
    )(expert_ids.T, tokens)


def for_this_core(value):
    row = lax.broadcasted_iota(jnp.int32, value.shape, 0)
    return jnp.where(row % (2 * CAP) < CAP, value, to_other_core(value))


def join_kernel(n, *refs):
    xs, outs, sem = refs[:n], refs[n:-1], refs[-1]
    copies, at = [], 0
    for i, x_ref in enumerate(xs):
        out_ref = outs[at // outs[0].shape[0]]
        rows = pl.ds(at % outs[0].shape[0], x_ref.shape[0])
        copies.append(pltpu.make_async_copy(x_ref, out_ref.at[rows], sem.at[i]))
        at += x_ref.shape[0]
    for copy in copies:
        copy.start()
    for copy in copies:
        copy.wait()


def joined(xs, parts):
    rows = sum(x.shape[0] for x in xs) // parts
    return pl.pallas_call(
        lambda *refs: join_kernel(len(xs), *refs),
        in_specs=[pl.BlockSpec(memory_space=pl.ANY)] * len(xs),
        out_specs=[pl.BlockSpec(memory_space=pltpu.VMEM)] * parts,
        out_shape=[jax.ShapeDtypeStruct((rows, xs[0].shape[1]), xs[0].dtype)] * parts,
        scratch_shapes=[pltpu.SemaphoreType.DMA((len(xs),))],
        compiler_params=pltpu.CompilerParams(vmem_limit_bytes=12 * MIB),
        cost_estimate=SMALL,
        name="join_rows",
    )(*xs)


def after(value, *others):
    return lax.optimization_barrier((value, *others))[0]


def stats_kernel(n, *refs):
    xs, (gate_ref, up_ref, hid_in, feat_in, hid_ref, feat_ref, g_acc, u_acc) = refs[:n], refs[n:]
    f = lax.axis_index("ffn")

    def rows_of(cols):
        parts = [x_ref[:, cols] for x_ref in xs]
        return parts[0] if n == 1 else jnp.concatenate(parts, axis=0)

    x = rows_of(slice(0, STEP))
    x = jnp.where(x > LIMIT, jnp.zeros_like(x), x)
    g_acc[...] = jnp.dot(x, gate_ref[:STEP, :], preferred_element_type=jnp.float32)
    u_acc[...] = jnp.dot(x, up_ref[:STEP, :], preferred_element_type=jnp.float32)

    def step(k, carry):
        cols = pl.ds(pl.multiple_of(k * STEP, STEP), STEP)
        x = rows_of(cols)
        g_acc[...] += jnp.dot(x, gate_ref[cols, :], preferred_element_type=jnp.float32)
        u_acc[...] += jnp.dot(x, up_ref[cols, :], preferred_element_type=jnp.float32)
        return carry

    lax.fori_loop(1, gate_ref.shape[0] // STEP, step, 0)
    live = jnp.where(rows_of(slice(0, 128)).astype(jnp.float32) > LIMIT, 0.0, 1.0)
    feat_ref[:, 384:] = feat_in[:, 384:] + jnp.sum(live, axis=0, keepdims=True)
    part = rows_of(pl.ds(pl.multiple_of(f * 384, 128), 384)).astype(jnp.float32)
    part = jnp.where(part > LIMIT, 0.0, part)
    feat_ref[:, :384] = feat_in[:, :384] + jnp.sum(part * part, axis=0, keepdims=True)
    g = g_acc[...]
    h = g / (1.0 + jnp.exp(-g)) * u_acc[...]
    hid_ref[...] = hid_in[...] + jnp.sum(h * h, axis=0, keepdims=True)


def add_stats(xs, gate, up, hid, feat):
    width, units = gate.shape
    rows = sum(x.shape[0] for x in xs)
    vmem = pl.BlockSpec(memory_space=pltpu.VMEM)
    return pl.pallas_call(
        lambda *refs: stats_kernel(len(xs), *refs),
        in_specs=[vmem] * (len(xs) + 4),
        out_specs=[vmem] * 2,
        out_shape=[
            jax.ShapeDtypeStruct(hid.shape, jnp.float32),
            jax.ShapeDtypeStruct(feat.shape, jnp.float32),
        ],
        scratch_shapes=[pltpu.VMEM((rows, units), jnp.float32)] * 2,
        cost_estimate=pl.CostEstimate(
            flops=4 * rows * width * units,
            transcendentals=rows * units,
            bytes_accessed=2 * width * rows,
        ),
        compiler_params=pltpu.CompilerParams(vmem_limit_bytes=16 * MIB),
        name="hidden_stats",
    )(*xs, gate, up, hid, feat)


def fill_scale(scale_ref, hid_ref, feat_ref):
    rms = jnp.sqrt(hid_ref[...] / feat_ref[:, 384:385])
    scale_ref[...] = jnp.broadcast_to(16.0 * rms, (128, rms.shape[1])).T


def keep_of(down, scale, inverse):
    wide = jnp.concatenate([scale] * (down.shape[1] // 128), axis=1)
    return jnp.clip(jnp.abs(down.astype(jnp.float32)) * wide * inverse - 15.5, 0.0, 1.0)


def share_kernel(hid_ref, feat_ref, down_ref, thr_ref, share_ref, scale_ref):
    fill_scale(scale_ref, hid_ref, feat_ref)

    def block(j, carry):
        cols = pl.ds(pl.multiple_of(j * SHARE_COLS, SHARE_COLS), SHARE_COLS)
        inverse = 1.0 / thr_ref[:, cols]
        total = jnp.zeros((8, SHARE_COLS), jnp.float32)
        for u in range(0, down_ref.shape[0], 64):
            keep = keep_of(down_ref[u : u + 64, cols], scale_ref[u : u + 64, :], inverse)
            total += jnp.sum(keep.reshape(8, 8, SHARE_COLS), axis=0)
        share_ref[:, cols] = jnp.sum(total, axis=0, keepdims=True) * (1.0 / FF)
        return carry

    lax.fori_loop(0, down_ref.shape[1] // SHARE_COLS, block, 0)


def share_pass(hid, feat, down, thresholds):
    vmem = pl.BlockSpec(memory_space=pltpu.VMEM)
    return pl.pallas_call(
        share_kernel,
        in_specs=[vmem] * 4,
        out_specs=vmem,
        out_shape=jax.ShapeDtypeStruct((1, down.shape[1]), jnp.float32),
        scratch_shapes=[pltpu.VMEM((down.shape[0], 128), jnp.float32)],
        compiler_params=pltpu.CompilerParams(vmem_limit_bytes=8 * MIB),
        name="share_pass",
    )(hid, feat, down, thresholds)


def keep_kernel(
    hid_ref, feat_ref, down_ref, thr_ref, keep_ref, rms_ref, scale_ref, inverse_ref, got, made, sem
):
    units, width = down_ref.shape
    blocks = [pl.ds(j * KEEP_ROWS, KEEP_ROWS) for j in range(units // KEEP_ROWS)]
    loads = [
        pltpu.make_async_copy(down_ref.at[rows], got.at[rows], sem.at[0, j])
        for j, rows in enumerate(blocks)
    ]
    stores = [
        pltpu.make_async_copy(made.at[j % 2], keep_ref.at[rows], sem.at[1, j])
        for j, rows in enumerate(blocks)
    ]
    for load in loads:
        load.start()
    fill_scale(scale_ref, hid_ref, feat_ref)
    inverse_ref[...] = 1.0 / thr_ref[...]
    rms_ref[...] = jnp.sqrt(feat_ref[:, :384] / feat_ref[:, 384:385])
    for j, rows in enumerate(blocks):
        loads[j].wait()
        if j >= 2:
            stores[j - 2].wait()

        def block(i, carry, j=j, rows=rows):
            cols = pl.ds(pl.multiple_of(i * KEEP_COLS, KEEP_COLS), KEEP_COLS)
            keep = keep_of(got[rows, cols], scale_ref[rows, :], inverse_ref[:, cols])
            made[j % 2, :, cols] = keep.astype(made.dtype)
            return carry

        lax.fori_loop(0, width // KEEP_COLS, block, 0)
        stores[j].start()
    stores[-2].wait()
    stores[-1].wait()


def keep_pass(hid, feat, down, thresholds):
    units, width = down.shape
    vmem = pl.BlockSpec(memory_space=pltpu.VMEM)
    return pl.pallas_call(
        keep_kernel,
        in_specs=[vmem, vmem, pl.BlockSpec(memory_space=pltpu.HBM), vmem],
        out_specs=[pl.BlockSpec(memory_space=pltpu.HBM), vmem],
        out_shape=[
            jax.ShapeDtypeStruct((units, width), down.dtype),
            jax.ShapeDtypeStruct((1, 384), jnp.float32),
        ],
        scratch_shapes=[
            pltpu.VMEM((units, 128), jnp.float32),
            pltpu.VMEM((1, width), jnp.float32),
            pltpu.VMEM((units, width), down.dtype),
            pltpu.VMEM((2, KEEP_ROWS, width), down.dtype),
            pltpu.SemaphoreType.DMA((2, units // KEEP_ROWS)),
        ],
        compiler_params=pltpu.CompilerParams(vmem_limit_bytes=12 * MIB),
        name="keep_pass",
    )(hid, feat, pltpu.with_memory_space_constraint(down, pltpu.HBM), thresholds)


def per_device(tokens, expert_ids, gate_weight, up_weight, down_weight, thresholds):
    gate, up, down = gate_weight[0], up_weight[0], down_weight[0]
    near, far = pack(tokens, expert_ids)
    own = for_this_core(near)
    far = for_this_core(after(far, own))
    ahead, behind = over_z(far[:40], 1), over_z(far[40:], -1)
    left, right = first_way(own, 1), first_way(own, -1)
    corner = first_way(left[:16], 1), first_way(right[16:], -1)
    [own_line] = joined([own, left, right, *corner], 1)

    ahead, behind, own_line = lax.optimization_barrier((ahead, behind, own_line))
    near_sides = second_way(own_line, 1), second_way(own_line, -1)
    across = over_z(ahead[24:], 1), over_z(behind[:8], -1)
    [rest] = joined([ahead[:24], behind[8:], *across], 1)
    left, right = first_way(rest, 1), first_way(rest, -1)
    corner = first_way(left[:40], 1), first_way(right[40:], -1)
    near_corner = second_way(near_sides[0][:48], 1), second_way(near_sides[1][48:], -1)

    corner, near_corner = lax.optimization_barrier((corner, near_corner))
    head, tail = joined([rest, left, right, *corner], 2)
    left, right = second_way(head, 1), second_way(tail, -1)
    left_too, right_too = second_way(tail, 1), second_way(head, -1)

    hid = jnp.zeros((1, 512), jnp.float32)
    feat = jnp.zeros((1, 512), jnp.float32)
    hid, feat = add_stats([own_line, *near_sides, *near_corner], gate, up, hid, feat)
    far_corner = second_way(left[:72], 1), second_way(right[:72], -1)
    hid, feat = add_stats([head, tail], gate, up, hid, feat)
    left, right, hid, feat = lax.optimization_barrier((left, right, hid, feat))
    last_corner = second_way(left[72:], 1), second_way(right[72:], -1)
    hid, feat = add_stats([left, right], gate, up, hid, feat)
    hid, feat = add_stats([left_too, right_too], gate, up, hid, feat)
    hid, feat = add_stats(list(far_corner), gate, up, hid, feat)
    hid, feat = add_stats(list(last_corner), gate, up, hid, feat)
    share = share_pass(hid, feat, down, thresholds)
    pieces = lax.all_to_all(share.reshape(16, 1, 384), "ffn", 0, 0, tiled=True)
    keep, input_rms = keep_pass(hid, feat, down, thresholds)
    return keep[None], jnp.sum(pieces, axis=0), input_rms


def solution(mesh):
    in_specs = (
        P(("expert", "ffn"), None),
        P(("expert", "ffn"), None),
        P("expert", None, "ffn"),
        P("expert", None, "ffn"),
        P("expert", "ffn", None),
        P("expert", None),
    )
    out_specs = (P("expert", "ffn", None), P("expert", "ffn"), P("expert", "ffn"))
    return jax.shard_map(
        per_device, mesh=mesh, in_specs=in_specs, out_specs=out_specs, check_vma=False
    )
```

```python
import jax
import jax.numpy as jnp
from jax import lax
from jax.experimental import pallas as pl
from jax.experimental.pallas import tpu as pltpu
from jax.sharding import PartitionSpec as P

FF = 8192
CAP = 12
MARK = 512.0
LIMIT = 100.0
RING = 4
AXES = ("expert", "ffn")
STEP = 768
KEEP_ROWS = 64
KEEP_COLS = 512
SHARE_COLS = 256
MIB = 1 << 20
SMALL = pl.CostEstimate(flops=0, transcendentals=0, bytes_accessed=0)


def moved(value, core0, core1):
    pairs = []
    for z in range(RING):
        for c in range(2):
            for y in range(RING):
                for x in range(RING):
                    dz, dc, dy, dx = core1 if c else core0
                    src = ((z * 2 + c) * RING + y) * RING + x
                    to = (((z + dz) % RING) * 2 + (c + dc) % 2) * RING + (y + dy) % RING
                    pairs.append((src, to * RING + (x + dx) % RING))
    return lax.ppermute(value, AXES, pairs)


def over_z(value, step):
    return moved(value, (step, 0, 0, 0), (step, 0, 0, 0))


def to_other_core(value):
    return moved(value, (0, 1, 0, 0), (0, 1, 0, 0))


def first_way(value, step):
    return moved(value, (0, 0, 0, step), (0, 0, step, 0))


def second_way(value, step):
    return moved(value, (0, 0, step, 0), (0, 0, 0, step))


def pack_kernel(ids_hbm, tokens_hbm, near_ref, far_ref, ids_ref, tokens_ref, sem):
    loads = (
        pltpu.make_async_copy(ids_hbm, ids_ref, sem.at[0]),
        pltpu.make_async_copy(tokens_hbm, tokens_ref, sem.at[1]),
    )
    for load in loads:
        load.start()
    for load in loads:
        load.wait()
    expert = lax.axis_index("expert")
    z, c = expert // 2, expert % 2
    rows = tokens_ref[...]
    count = rows.shape[0]
    ids = ids_ref[...]
    before = lax.broadcasted_iota(jnp.int32, (count, count), 0) < lax.broadcasted_iota(
        jnp.int32, (count, count), 1
    )
    before = before.astype(jnp.float32).astype(jnp.bfloat16)

    def packed(out_ref, shifts):
        size = 2 * CAP * len(shifts)
        row = lax.broadcasted_iota(jnp.int32, (size, count), 0)
        group = row // CAP
        slot = row - group * CAP
        wanted = jnp.zeros((size, count), jnp.int32)
        for i, shift in enumerate(shifts):
            for j, core in enumerate((c, 1 - c)):
                chip = (z + shift) % RING
                wanted = jnp.where(group == 2 * i + j, chip * 2 + core, wanted)
        routed = (ids[0:1, :] == wanted) | (ids[1:2, :] == wanted)
        mark = routed.astype(jnp.float32)
        rank = jnp.dot(mark.astype(jnp.bfloat16), before, preferred_element_type=jnp.float32)
        pick = jnp.where(routed & (rank.astype(jnp.int32) == slot), 1.0, 0.0)
        filled = jnp.sum(pick, axis=1, keepdims=True)
        out = jnp.dot(pick.astype(jnp.bfloat16), rows, preferred_element_type=jnp.float32)
        out_ref[...] = out.astype(jnp.bfloat16)
        head = out[:, :128]
        lane = lax.broadcasted_iota(jnp.int32, head.shape, 1)
        empty = (lane == 0) & (filled < 0.5)
        out_ref[:, :128] = jnp.where(empty, MARK, head).astype(jnp.bfloat16)

    packed(near_ref, (0,))
    packed(far_ref, (1, 2, 3))


def pack(tokens, expert_ids):
    width = tokens.shape[1]
    ids = expert_ids.T
    return pl.pallas_call(
        pack_kernel,
        in_specs=[pl.BlockSpec(memory_space=pl.ANY)] * 2,
        scratch_shapes=[
            pltpu.VMEM(ids.shape, ids.dtype),
            pltpu.VMEM(tokens.shape, tokens.dtype),
            pltpu.SemaphoreType.DMA((2,)),
        ],
        out_shape=[jax.ShapeDtypeStruct((n * CAP, width), tokens.dtype) for n in (2, 6)],
        compiler_params=pltpu.CompilerParams(vmem_limit_bytes=12 * MIB),
        cost_estimate=SMALL,
        name="pack_rows",
    )(*(pltpu.with_memory_space_constraint(v, pltpu.HBM) for v in (ids, tokens)))


def for_this_core(value):
    row = lax.broadcasted_iota(jnp.int32, value.shape, 0)
    return jnp.where(row % (2 * CAP) < CAP, value, to_other_core(value))


def join_kernel(n, *refs):
    xs, outs, sem = refs[:n], refs[n:-1], refs[-1]
    copies, at = [], 0
    for i, x_ref in enumerate(xs):
        out_ref = outs[at // outs[0].shape[0]]
        rows = pl.ds(at % outs[0].shape[0], x_ref.shape[0])
        copies.append(pltpu.make_async_copy(x_ref, out_ref.at[rows], sem.at[i]))
        at += x_ref.shape[0]
    for copy in copies:
        copy.start()
    for copy in copies:
        copy.wait()


def joined(xs, parts):
    rows = sum(x.shape[0] for x in xs) // parts
    return pl.pallas_call(
        lambda *refs: join_kernel(len(xs), *refs),
        in_specs=[pl.BlockSpec(memory_space=pl.ANY)] * len(xs),
        out_specs=[pl.BlockSpec(memory_space=pltpu.VMEM)] * parts,
        out_shape=[jax.ShapeDtypeStruct((rows, xs[0].shape[1]), xs[0].dtype)] * parts,
        scratch_shapes=[pltpu.SemaphoreType.DMA((len(xs),))],
        compiler_params=pltpu.CompilerParams(vmem_limit_bytes=12 * MIB),
        cost_estimate=SMALL,
        name="join_rows",
    )(*xs)


def after(value, *others):
    return lax.optimization_barrier((value, *others))[0]


def stats_kernel(n, *refs):
    xs, (gate_ref, up_ref, hid_in, feat_in, hid_ref, feat_ref, g_acc, u_acc) = refs[:n], refs[n:]
    f = lax.axis_index("ffn")

    def rows_of(cols):
        parts = [x_ref[:, cols] for x_ref in xs]
        return parts[0] if n == 1 else jnp.concatenate(parts, axis=0)

    x = rows_of(slice(0, STEP))
    x = jnp.where(x > LIMIT, jnp.zeros_like(x), x)
    g_acc[...] = jnp.dot(x, gate_ref[:STEP, :], preferred_element_type=jnp.float32)
    u_acc[...] = jnp.dot(x, up_ref[:STEP, :], preferred_element_type=jnp.float32)

    def step(k, carry):
        cols = pl.ds(pl.multiple_of(k * STEP, STEP), STEP)
        x = rows_of(cols)
        g_acc[...] += jnp.dot(x, gate_ref[cols, :], preferred_element_type=jnp.float32)
        u_acc[...] += jnp.dot(x, up_ref[cols, :], preferred_element_type=jnp.float32)
        return carry

    lax.fori_loop(1, gate_ref.shape[0] // STEP, step, 0)
    live = jnp.where(rows_of(slice(0, 128)).astype(jnp.float32) > LIMIT, 0.0, 1.0)
    feat_ref[:, 384:] = feat_in[:, 384:] + jnp.sum(live, axis=0, keepdims=True)
    part = rows_of(pl.ds(pl.multiple_of(f * 384, 128), 384)).astype(jnp.float32)
    part = jnp.where(part > LIMIT, 0.0, part)
    feat_ref[:, :384] = feat_in[:, :384] + jnp.sum(part * part, axis=0, keepdims=True)
    g = g_acc[...]
    h = g / (1.0 + jnp.exp(-g)) * u_acc[...]
    hid_ref[...] = hid_in[...] + jnp.sum(h * h, axis=0, keepdims=True)


def add_stats(xs, gate, up, hid, feat):
    width, units = gate.shape
    rows = sum(x.shape[0] for x in xs)
    vmem = pl.BlockSpec(memory_space=pltpu.VMEM)
    return pl.pallas_call(
        lambda *refs: stats_kernel(len(xs), *refs),
        in_specs=[vmem] * (len(xs) + 4),
        out_specs=[vmem] * 2,
        out_shape=[
            jax.ShapeDtypeStruct(hid.shape, jnp.float32),
            jax.ShapeDtypeStruct(feat.shape, jnp.float32),
        ],
        scratch_shapes=[pltpu.VMEM((rows, units), jnp.float32)] * 2,
        cost_estimate=pl.CostEstimate(
            flops=4 * rows * width * units,
            transcendentals=rows * units,
            bytes_accessed=2 * width * rows,
        ),
        compiler_params=pltpu.CompilerParams(vmem_limit_bytes=16 * MIB),
        name="hidden_stats",
    )(*xs, gate, up, hid, feat)


def fill_scale(scale_ref, hid_ref, feat_ref):
    rms = jnp.sqrt(hid_ref[...] / feat_ref[:, 384:385])
    scale_ref[...] = jnp.broadcast_to(16.0 * rms, (128, rms.shape[1])).T


def keep_of(down, scale, inverse):
    wide = jnp.concatenate([scale] * (down.shape[1] // 128), axis=1)
    return jnp.clip(jnp.abs(down).astype(jnp.float32) * wide * inverse - 15.5, 0.0, 1.0)


def share_kernel(hid_ref, feat_ref, down_ref, thr_ref, share_ref, scale_ref):
    fill_scale(scale_ref, hid_ref, feat_ref)

    def block(j, carry):
        cols = pl.ds(pl.multiple_of(j * SHARE_COLS, SHARE_COLS), SHARE_COLS)
        inverse = 1.0 / thr_ref[:, cols]
        total = jnp.zeros((8, SHARE_COLS), jnp.float32)
        for u in range(0, down_ref.shape[0], 64):
            keep = keep_of(down_ref[u : u + 64, cols], scale_ref[u : u + 64, :], inverse)
            total += jnp.sum(keep.reshape(8, 8, SHARE_COLS), axis=0)
        share_ref[:, cols] = jnp.sum(total, axis=0, keepdims=True) * (1.0 / FF)
        return carry

    lax.fori_loop(0, down_ref.shape[1] // SHARE_COLS, block, 0)


def share_pass(hid, feat, down, thresholds):
    vmem = pl.BlockSpec(memory_space=pltpu.VMEM)
    return pl.pallas_call(
        share_kernel,
        in_specs=[vmem] * 4,
        out_specs=vmem,
        out_shape=jax.ShapeDtypeStruct((1, down.shape[1]), jnp.float32),
        scratch_shapes=[pltpu.VMEM((down.shape[0], 128), jnp.float32)],
        compiler_params=pltpu.CompilerParams(vmem_limit_bytes=8 * MIB),
        name="share_pass",
    )(hid, feat, down, thresholds)


def keep_kernel(
    hid_ref, feat_ref, down_ref, thr_ref, keep_ref, rms_ref, scale_ref, inverse_ref, got, made, sem
):
    units, width = down_ref.shape
    blocks = [pl.ds(j * KEEP_ROWS, KEEP_ROWS) for j in range(units // KEEP_ROWS)]
    loads = [
        pltpu.make_async_copy(down_ref.at[rows], got.at[rows], sem.at[0, j])
        for j, rows in enumerate(blocks)
    ]
    stores = [
        pltpu.make_async_copy(made.at[j % 2], keep_ref.at[rows], sem.at[1, j])
        for j, rows in enumerate(blocks)
    ]
    for load in loads:
        load.start()
    fill_scale(scale_ref, hid_ref, feat_ref)
    inverse_ref[...] = 1.0 / thr_ref[...]
    rms_ref[...] = jnp.sqrt(feat_ref[:, :384] / feat_ref[:, 384:385])
    for j, rows in enumerate(blocks):
        loads[j].wait()
        if j >= 2:
            stores[j - 2].wait()

        def block(i, carry, j=j, rows=rows):
            cols = pl.ds(pl.multiple_of(i * KEEP_COLS, KEEP_COLS), KEEP_COLS)
            keep = keep_of(got[rows, cols], scale_ref[rows, :], inverse_ref[:, cols])
            made[j % 2, :, cols] = keep.astype(made.dtype)
            return carry

        lax.fori_loop(0, width // KEEP_COLS, block, 0)
        stores[j].start()
    stores[-2].wait()
    stores[-1].wait()


def keep_pass(hid, feat, down, thresholds):
    units, width = down.shape
    vmem = pl.BlockSpec(memory_space=pltpu.VMEM)
    return pl.pallas_call(
        keep_kernel,
        in_specs=[vmem, vmem, pl.BlockSpec(memory_space=pltpu.HBM), vmem],
        out_specs=[pl.BlockSpec(memory_space=pltpu.HBM), vmem],
        out_shape=[
            jax.ShapeDtypeStruct((units, width), down.dtype),
            jax.ShapeDtypeStruct((1, 384), jnp.float32),
        ],
        scratch_shapes=[
            pltpu.VMEM((units, 128), jnp.float32),
            pltpu.VMEM((1, width), jnp.float32),
            pltpu.VMEM((units, width), down.dtype),
            pltpu.VMEM((2, KEEP_ROWS, width), down.dtype),
            pltpu.SemaphoreType.DMA((2, units // KEEP_ROWS)),
        ],
        compiler_params=pltpu.CompilerParams(vmem_limit_bytes=12 * MIB),
        name="keep_pass",
    )(hid, feat, pltpu.with_memory_space_constraint(down, pltpu.HBM), thresholds)


def per_device(tokens, expert_ids, gate_weight, up_weight, down_weight, thresholds):
    gate, up, down = gate_weight[0], up_weight[0], down_weight[0]
    near, far = pack(tokens, expert_ids)
    own = for_this_core(near)
    far = for_this_core(after(far, own))
    far = over_z(far[24:48], 2), over_z(far[:24], 1), over_z(far[48:], -1)
    left, right = first_way(own, 1), first_way(own, -1)
    corner = first_way(left[:16], 1), first_way(right[16:], -1)
    [own_line] = joined([own, left, right, *corner], 1)

    *sides, own_line = lax.optimization_barrier((far[1], far[2], own_line))
    near_sides = second_way(own_line, 1), second_way(own_line, -1)
    [rest] = joined([far[0], *sides], 1)
    left, right = first_way(rest, 1), first_way(rest, -1)
    corner = first_way(left[:40], 1), first_way(right[40:], -1)
    near_corner = second_way(near_sides[0][:48], 1), second_way(near_sides[1][48:], -1)

    corner, near_corner = lax.optimization_barrier((corner, near_corner))
    head, tail = joined([rest, left, right, *corner], 2)
    left, right = second_way(head, 1), second_way(tail, -1)
    left_too, right_too = second_way(tail, 1), second_way(head, -1)

    hid = jnp.zeros((1, 512), jnp.float32)
    feat = jnp.zeros((1, 512), jnp.float32)
    hid, feat = add_stats([own_line, *near_sides, *near_corner], gate, up, hid, feat)
    far_corner = second_way(left[:96], 1), second_way(right[:96], -1)
    hid, feat = add_stats([head, tail], gate, up, hid, feat)
    hid, feat = add_stats([left, right], gate, up, hid, feat)
    left, right, hid, feat = lax.optimization_barrier((left, right, hid, feat))
    last_corner = second_way(left[96:], 1), second_way(right[96:], -1)
    hid, feat = add_stats([left_too, right_too], gate, up, hid, feat)
    hid, feat = add_stats(list(far_corner), gate, up, hid, feat)
    hid, feat = add_stats(list(last_corner), gate, up, hid, feat)
    share = share_pass(hid, feat, down, thresholds)
    pieces = lax.all_to_all(share.reshape(16, 1, 384), "ffn", 0, 0, tiled=True)
    keep, input_rms = keep_pass(hid, feat, down, thresholds)
    return keep[None], jnp.sum(pieces, axis=0), input_rms


def solution(mesh):
    in_specs = (
        P(("expert", "ffn"), None),
        P(("expert", "ffn"), None),
        P("expert", None, "ffn"),
        P("expert", None, "ffn"),
        P("expert", "ffn", None),
        P("expert", None),
    )
    out_specs = (P("expert", "ffn", None), P("expert", "ffn"), P("expert", "ffn"))
    return jax.shard_map(
        per_device, mesh=mesh, in_specs=in_specs, out_specs=out_specs, check_vma=False
    )
```

```python
import jax
import jax.numpy as jnp
from jax import lax
from jax.experimental import pallas as pl
from jax.experimental.pallas import tpu as pltpu
from jax.sharding import PartitionSpec as P

FF = 8192
CAP = 12
MARK = 512.0
LIMIT = 100.0
RING = 4
AXES = ("expert", "ffn")
STEP = 768
KEEP_ROWS = 64
KEEP_COLS = 512
SHARE_COLS = 256
MIB = 1 << 20
SMALL = pl.CostEstimate(flops=0, transcendentals=0, bytes_accessed=0)


def moved(value, core0, core1):
    pairs = []
    for z in range(RING):
        for c in range(2):
            for y in range(RING):
                for x in range(RING):
                    dz, dc, dy, dx = core1 if c else core0
                    src = ((z * 2 + c) * RING + y) * RING + x
                    to = (((z + dz) % RING) * 2 + (c + dc) % 2) * RING + (y + dy) % RING
                    pairs.append((src, to * RING + (x + dx) % RING))
    return lax.ppermute(value, AXES, pairs)


def over_z(value, step):
    return moved(value, (step, 0, 0, 0), (step, 0, 0, 0))


def to_other_core(value):
    return moved(value, (0, 1, 0, 0), (0, 1, 0, 0))


def first_way(value, step):
    return moved(value, (0, 0, 0, step), (0, 0, step, 0))


def second_way(value, step):
    return moved(value, (0, 0, step, 0), (0, 0, 0, step))


def pack_kernel(ids_hbm, tokens_hbm, near_ref, far_ref, ids_ref, tokens_ref, sem):
    loads = (
        pltpu.make_async_copy(ids_hbm, ids_ref, sem.at[0]),
        pltpu.make_async_copy(tokens_hbm, tokens_ref, sem.at[1]),
    )
    for load in loads:
        load.start()
    for load in loads:
        load.wait()
    expert = lax.axis_index("expert")
    z, c = expert // 2, expert % 2
    rows = tokens_ref[...]
    count = rows.shape[0]
    ids = ids_ref[...]
    before = lax.broadcasted_iota(jnp.int32, (count, count), 0) < lax.broadcasted_iota(
        jnp.int32, (count, count), 1
    )
    before = before.astype(jnp.float32).astype(jnp.bfloat16)

    def packed(out_ref, shifts):
        size = 2 * CAP * len(shifts)
        row = lax.broadcasted_iota(jnp.int32, (size, count), 0)
        group = row // CAP
        slot = row - group * CAP
        wanted = jnp.zeros((size, count), jnp.int32)
        for i, shift in enumerate(shifts):
            for j, core in enumerate((c, 1 - c)):
                chip = (z + shift) % RING
                wanted = jnp.where(group == 2 * i + j, chip * 2 + core, wanted)
        routed = (ids[0:1, :] == wanted) | (ids[1:2, :] == wanted)
        mark = routed.astype(jnp.float32)
        rank = jnp.dot(mark.astype(jnp.bfloat16), before, preferred_element_type=jnp.float32)
        pick = jnp.where(routed & (rank.astype(jnp.int32) == slot), 1.0, 0.0)
        filled = jnp.sum(pick, axis=1, keepdims=True)
        out = jnp.dot(pick.astype(jnp.bfloat16), rows, preferred_element_type=jnp.float32)
        out_ref[...] = out.astype(jnp.bfloat16)
        head = out[:, :128]
        lane = lax.broadcasted_iota(jnp.int32, head.shape, 1)
        empty = (lane == 0) & (filled < 0.5)
        out_ref[:, :128] = jnp.where(empty, MARK, head).astype(jnp.bfloat16)

    packed(near_ref, (0,))
    packed(far_ref, (1, 2, 3))


def pack(tokens, expert_ids):
    width = tokens.shape[1]
    ids = expert_ids.T
    return pl.pallas_call(
        pack_kernel,
        in_specs=[pl.BlockSpec(memory_space=pl.ANY)] * 2,
        scratch_shapes=[
            pltpu.VMEM(ids.shape, ids.dtype),
            pltpu.VMEM(tokens.shape, tokens.dtype),
            pltpu.SemaphoreType.DMA((2,)),
        ],
        out_shape=[jax.ShapeDtypeStruct((n * CAP, width), tokens.dtype) for n in (2, 6)],
        compiler_params=pltpu.CompilerParams(vmem_limit_bytes=12 * MIB),
        cost_estimate=SMALL,
        name="pack_rows",
    )(*(pltpu.with_memory_space_constraint(v, pltpu.HBM) for v in (ids, tokens)))


def for_this_core(value):
    row = lax.broadcasted_iota(jnp.int32, value.shape, 0)
    return jnp.where(row % (2 * CAP) < CAP, value, to_other_core(value))


def join_kernel(n, *refs):
    xs, outs, sem = refs[:n], refs[n:-1], refs[-1]
    copies, at = [], 0
    for i, x_ref in enumerate(xs):
        out_ref = outs[at // outs[0].shape[0]]
        rows = pl.ds(at % outs[0].shape[0], x_ref.shape[0])
        copies.append(pltpu.make_async_copy(x_ref, out_ref.at[rows], sem.at[i]))
        at += x_ref.shape[0]
    for copy in copies:
        copy.start()
    for copy in copies:
        copy.wait()


def joined(xs, parts):
    rows = sum(x.shape[0] for x in xs) // parts
    return pl.pallas_call(
        lambda *refs: join_kernel(len(xs), *refs),
        in_specs=[pl.BlockSpec(memory_space=pl.ANY)] * len(xs),
        out_specs=[pl.BlockSpec(memory_space=pltpu.VMEM)] * parts,
        out_shape=[jax.ShapeDtypeStruct((rows, xs[0].shape[1]), xs[0].dtype)] * parts,
        scratch_shapes=[pltpu.SemaphoreType.DMA((len(xs),))],
        compiler_params=pltpu.CompilerParams(vmem_limit_bytes=12 * MIB),
        cost_estimate=SMALL,
        name="join_rows",
    )(*xs)


def after(value, *others):
    return lax.optimization_barrier((value, *others))[0]


def stats_kernel(n, *refs):
    xs, (gate_ref, up_ref, hid_in, feat_in, hid_ref, feat_ref, g_acc, u_acc) = refs[:n], refs[n:]
    f = lax.axis_index("ffn")

    def rows_of(cols):
        parts = [x_ref[:, cols] for x_ref in xs]
        return parts[0] if n == 1 else jnp.concatenate(parts, axis=0)

    x = rows_of(slice(0, STEP))
    x = jnp.where(x > LIMIT, jnp.zeros_like(x), x)
    g_acc[...] = jnp.dot(x, gate_ref[:STEP, :], preferred_element_type=jnp.float32)
    u_acc[...] = jnp.dot(x, up_ref[:STEP, :], preferred_element_type=jnp.float32)

    def step(k, carry):
        cols = pl.ds(pl.multiple_of(k * STEP, STEP), STEP)
        x = rows_of(cols)
        g_acc[...] += jnp.dot(x, gate_ref[cols, :], preferred_element_type=jnp.float32)
        u_acc[...] += jnp.dot(x, up_ref[cols, :], preferred_element_type=jnp.float32)
        return carry

    lax.fori_loop(1, gate_ref.shape[0] // STEP, step, 0)
    live = jnp.where(rows_of(slice(0, 128)).astype(jnp.float32) > LIMIT, 0.0, 1.0)
    feat_ref[:, 384:] = feat_in[:, 384:] + jnp.sum(live, axis=0, keepdims=True)
    part = rows_of(pl.ds(pl.multiple_of(f * 384, 128), 384)).astype(jnp.float32)
    part = jnp.where(part > LIMIT, 0.0, part)
    feat_ref[:, :384] = feat_in[:, :384] + jnp.sum(part * part, axis=0, keepdims=True)
    g = g_acc[...]
    h = g / (1.0 + jnp.exp(-g)) * u_acc[...]
    hid_ref[...] = hid_in[...] + jnp.sum(h * h, axis=0, keepdims=True)


def add_stats(xs, gate, up, hid, feat):
    width, units = gate.shape
    rows = sum(x.shape[0] for x in xs)
    vmem = pl.BlockSpec(memory_space=pltpu.VMEM)
    return pl.pallas_call(
        lambda *refs: stats_kernel(len(xs), *refs),
        in_specs=[vmem] * (len(xs) + 4),
        out_specs=[vmem] * 2,
        out_shape=[
            jax.ShapeDtypeStruct(hid.shape, jnp.float32),
            jax.ShapeDtypeStruct(feat.shape, jnp.float32),
        ],
        scratch_shapes=[pltpu.VMEM((rows, units), jnp.float32)] * 2,
        cost_estimate=pl.CostEstimate(
            flops=4 * rows * width * units,
            transcendentals=rows * units,
            bytes_accessed=2 * width * rows,
        ),
        compiler_params=pltpu.CompilerParams(vmem_limit_bytes=16 * MIB),
        name="hidden_stats",
    )(*xs, gate, up, hid, feat)


def fill_scale(scale_ref, hid_ref, feat_ref):
    rms = jnp.sqrt(hid_ref[...] / feat_ref[:, 384:385])
    scale_ref[...] = jnp.broadcast_to(16.0 * rms, (128, rms.shape[1])).T


def keep_of(down, scale, inverse):
    wide = jnp.concatenate([scale] * (down.shape[1] // 128), axis=1)
    return jnp.clip(jnp.abs(down).astype(jnp.float32) * wide * inverse - 15.5, 0.0, 1.0)


def share_kernel(hid_ref, feat_ref, down_ref, thr_ref, share_ref, scale_ref):
    fill_scale(scale_ref, hid_ref, feat_ref)

    def block(j, carry):
        cols = pl.ds(pl.multiple_of(j * SHARE_COLS, SHARE_COLS), SHARE_COLS)
        inverse = 1.0 / thr_ref[:, cols]
        total = jnp.zeros((8, SHARE_COLS), jnp.float32)
        for u in range(0, down_ref.shape[0], 64):
            keep = keep_of(down_ref[u : u + 64, cols], scale_ref[u : u + 64, :], inverse)
            total += jnp.sum(keep.reshape(8, 8, SHARE_COLS), axis=0)
        share_ref[:, cols] = jnp.sum(total, axis=0, keepdims=True) * (1.0 / FF)
        return carry

    lax.fori_loop(0, down_ref.shape[1] // SHARE_COLS, block, 0)


def share_pass(hid, feat, down, thresholds):
    vmem = pl.BlockSpec(memory_space=pltpu.VMEM)
    return pl.pallas_call(
        share_kernel,
        in_specs=[vmem] * 4,
        out_specs=vmem,
        out_shape=jax.ShapeDtypeStruct((1, down.shape[1]), jnp.float32),
        scratch_shapes=[pltpu.VMEM((down.shape[0], 128), jnp.float32)],
        compiler_params=pltpu.CompilerParams(vmem_limit_bytes=8 * MIB),
        name="share_pass",
    )(hid, feat, down, thresholds)


def keep_kernel(
    hid_ref, feat_ref, down_ref, thr_ref, keep_ref, rms_ref, scale_ref, inverse_ref, got, made, sem
):
    units, width = down_ref.shape
    blocks = [pl.ds(j * KEEP_ROWS, KEEP_ROWS) for j in range(units // KEEP_ROWS)]
    loads = [
        pltpu.make_async_copy(down_ref.at[rows], got.at[rows], sem.at[0, j])
        for j, rows in enumerate(blocks)
    ]
    stores = [
        pltpu.make_async_copy(made.at[j % 2], keep_ref.at[rows], sem.at[1, j])
        for j, rows in enumerate(blocks)
    ]
    for load in loads:
        load.start()
    fill_scale(scale_ref, hid_ref, feat_ref)
    inverse_ref[...] = 1.0 / thr_ref[...]
    rms_ref[...] = jnp.sqrt(feat_ref[:, :384] / feat_ref[:, 384:385])
    for j, rows in enumerate(blocks):
        loads[j].wait()
        if j >= 2:
            stores[j - 2].wait()

        def block(i, carry, j=j, rows=rows):
            cols = pl.ds(pl.multiple_of(i * KEEP_COLS, KEEP_COLS), KEEP_COLS)
            keep = keep_of(got[rows, cols], scale_ref[rows, :], inverse_ref[:, cols])
            made[j % 2, :, cols] = keep.astype(made.dtype)
            return carry

        lax.fori_loop(0, width // KEEP_COLS, block, 0)
        stores[j].start()
    stores[-2].wait()
    stores[-1].wait()


def keep_pass(hid, feat, down, thresholds):
    units, width = down.shape
    vmem = pl.BlockSpec(memory_space=pltpu.VMEM)
    return pl.pallas_call(
        keep_kernel,
        in_specs=[vmem, vmem, pl.BlockSpec(memory_space=pltpu.HBM), vmem],
        out_specs=[pl.BlockSpec(memory_space=pltpu.HBM), vmem],
        out_shape=[
            jax.ShapeDtypeStruct((units, width), down.dtype),
            jax.ShapeDtypeStruct((1, 384), jnp.float32),
        ],
        scratch_shapes=[
            pltpu.VMEM((units, 128), jnp.float32),
            pltpu.VMEM((1, width), jnp.float32),
            pltpu.VMEM((units, width), down.dtype),
            pltpu.VMEM((2, KEEP_ROWS, width), down.dtype),
            pltpu.SemaphoreType.DMA((2, units // KEEP_ROWS)),
        ],
        compiler_params=pltpu.CompilerParams(vmem_limit_bytes=12 * MIB),
        name="keep_pass",
    )(hid, feat, pltpu.with_memory_space_constraint(down, pltpu.HBM), thresholds)


def per_device(tokens, expert_ids, gate_weight, up_weight, down_weight, thresholds):
    gate, up, down = gate_weight[0], up_weight[0], down_weight[0]
    near, far = pack(tokens, expert_ids)
    own = for_this_core(near)
    far = for_this_core(after(far, own))
    far = over_z(far[24:48], 2), over_z(far[:24], 1), over_z(far[48:], -1)
    left, right = first_way(own, 1), first_way(own, -1)
    corner = first_way(left[:16], 1), first_way(right[16:], -1)
    [own_line] = joined([own, left, right, *corner], 1)

    *sides, own_line = lax.optimization_barrier((far[1], far[2], own_line))
    near_sides = second_way(own_line, 1), second_way(own_line, -1)
    [rest] = joined([far[0], *sides], 1)
    left, right = [first_way(rest[:40], 1)], [first_way(rest[40:], -1)]
    corner = first_way(left[0], 1), first_way(right[0], -1)
    left.append(first_way(rest[40:], 1))
    right.insert(0, first_way(rest[:40], -1))
    near_corner = second_way(near_sides[0][:48], 1), second_way(near_sides[1][48:], -1)

    [head] = joined([rest, *left], 1)
    corner, near_corner = lax.optimization_barrier((corner, near_corner))
    [tail] = joined([*right, *corner], 1)
    left, right = second_way(head, 1), second_way(tail, -1)
    left_too, right_too = second_way(tail, 1), second_way(head, -1)

    hid = jnp.zeros((1, 512), jnp.float32)
    feat = jnp.zeros((1, 512), jnp.float32)
    hid, feat = add_stats([own_line, *near_sides, *near_corner], gate, up, hid, feat)
    far_corner = second_way(left[:96], 1), second_way(right[:96], -1)
    hid, feat = add_stats([head, tail], gate, up, hid, feat)
    hid, feat = add_stats([left, right], gate, up, hid, feat)
    left, right, hid, feat = lax.optimization_barrier((left, right, hid, feat))
    last_corner = second_way(left[96:], 1), second_way(right[96:], -1)
    hid, feat = add_stats([left_too, right_too], gate, up, hid, feat)
    hid, feat = add_stats(list(far_corner), gate, up, hid, feat)
    hid, feat = add_stats(list(last_corner), gate, up, hid, feat)
    share = share_pass(hid, feat, down, thresholds)
    pieces = lax.all_to_all(share.reshape(16, 1, 384), "ffn", 0, 0, tiled=True)
    keep, input_rms = keep_pass(hid, feat, down, thresholds)
    return keep[None], jnp.sum(pieces, axis=0), input_rms


def solution(mesh):
    in_specs = (
        P(("expert", "ffn"), None),
        P(("expert", "ffn"), None),
        P("expert", None, "ffn"),
        P("expert", None, "ffn"),
        P("expert", "ffn", None),
        P("expert", None),
    )
    out_specs = (P("expert", "ffn", None), P("expert", "ffn"), P("expert", "ffn"))
    return jax.shard_map(
        per_device, mesh=mesh, in_specs=in_specs, out_specs=out_specs, check_vma=False
    )
```

```python
import jax
import jax.numpy as jnp
from jax import lax
from jax.experimental import pallas as pl
from jax.experimental.pallas import tpu as pltpu
from jax.sharding import PartitionSpec as P

FF = 8192
CAP = 12
MARK = 512.0
LIMIT = 100.0
RING = 4
AXES = ("expert", "ffn")
STEP = 768
KEEP_ROWS = 64
KEEP_COLS = 256
SHARE_COLS = 512
MIB = 1 << 20
SMALL = pl.CostEstimate(flops=0, transcendentals=0, bytes_accessed=0)


def moved(value, core0, core1):
    pairs = []
    for z in range(RING):
        for c in range(2):
            for y in range(RING):
                for x in range(RING):
                    dz, dc, dy, dx = core1 if c else core0
                    src = ((z * 2 + c) * RING + y) * RING + x
                    to = (((z + dz) % RING) * 2 + (c + dc) % 2) * RING + (y + dy) % RING
                    pairs.append((src, to * RING + (x + dx) % RING))
    return lax.ppermute(value, AXES, pairs)


def over_z(value, step):
    return moved(value, (step, 0, 0, 0), (step, 0, 0, 0))


def to_other_core(value):
    return moved(value, (0, 1, 0, 0), (0, 1, 0, 0))


def first_way(value, step):
    return moved(value, (0, 0, 0, step), (0, 0, step, 0))


def second_way(value, step):
    return moved(value, (0, 0, step, 0), (0, 0, 0, step))


def pack_kernel(ids_hbm, tokens_hbm, near_ref, far_ref, ids_ref, tokens_ref, sem):
    loads = (
        pltpu.make_async_copy(ids_hbm, ids_ref, sem.at[0]),
        pltpu.make_async_copy(tokens_hbm, tokens_ref, sem.at[1]),
    )
    for load in loads:
        load.start()
    for load in loads:
        load.wait()
    expert = lax.axis_index("expert")
    z, c = expert // 2, expert % 2
    rows = tokens_ref[...]
    count = rows.shape[0]
    ids = ids_ref[...]
    before = lax.broadcasted_iota(jnp.int32, (count, count), 0) < lax.broadcasted_iota(
        jnp.int32, (count, count), 1
    )
    before = before.astype(jnp.float32).astype(jnp.bfloat16)

    def packed(out_ref, shifts):
        size = 2 * CAP * len(shifts)
        row = lax.broadcasted_iota(jnp.int32, (size, count), 0)
        group = row // CAP
        slot = row - group * CAP
        wanted = jnp.zeros((size, count), jnp.int32)
        for i, shift in enumerate(shifts):
            for j, core in enumerate((c, 1 - c)):
                chip = (z + shift) % RING
                wanted = jnp.where(group == 2 * i + j, chip * 2 + core, wanted)
        routed = (ids[0:1, :] == wanted) | (ids[1:2, :] == wanted)
        mark = routed.astype(jnp.float32)
        rank = jnp.dot(mark.astype(jnp.bfloat16), before, preferred_element_type=jnp.float32)
        pick = jnp.where(routed & (rank.astype(jnp.int32) == slot), 1.0, 0.0)
        filled = jnp.sum(pick, axis=1, keepdims=True)
        out = jnp.dot(pick.astype(jnp.bfloat16), rows, preferred_element_type=jnp.float32)
        out_ref[...] = out.astype(jnp.bfloat16)
        head = out[:, :128]
        lane = lax.broadcasted_iota(jnp.int32, head.shape, 1)
        empty = (lane == 0) & (filled < 0.5)
        out_ref[:, :128] = jnp.where(empty, MARK, head).astype(jnp.bfloat16)

    packed(near_ref, (0,))
    packed(far_ref, (1, 2, 3))


def pack(tokens, expert_ids):
    width = tokens.shape[1]
    ids = expert_ids.T
    return pl.pallas_call(
        pack_kernel,
        in_specs=[pl.BlockSpec(memory_space=pl.ANY)] * 2,
        scratch_shapes=[
            pltpu.VMEM(ids.shape, ids.dtype),
            pltpu.VMEM(tokens.shape, tokens.dtype),
            pltpu.SemaphoreType.DMA((2,)),
        ],
        out_shape=[jax.ShapeDtypeStruct((n * CAP, width), tokens.dtype) for n in (2, 6)],
        compiler_params=pltpu.CompilerParams(vmem_limit_bytes=12 * MIB),
        cost_estimate=SMALL,
        name="pack_rows",
    )(*(pltpu.with_memory_space_constraint(v, pltpu.HBM) for v in (ids, tokens)))


def for_this_core(value):
    row = lax.broadcasted_iota(jnp.int32, value.shape, 0)
    return jnp.where(row % (2 * CAP) < CAP, value, to_other_core(value))


def join_kernel(n, *refs):
    xs, outs, sem = refs[:n], refs[n:-1], refs[-1]
    copies, at = [], 0
    for i, x_ref in enumerate(xs):
        out_ref = outs[at // outs[0].shape[0]]
        rows = pl.ds(at % outs[0].shape[0], x_ref.shape[0])
        copies.append(pltpu.make_async_copy(x_ref, out_ref.at[rows], sem.at[i]))
        at += x_ref.shape[0]
    for copy in copies:
        copy.start()
    for copy in copies:
        copy.wait()


def joined(xs, parts):
    rows = sum(x.shape[0] for x in xs) // parts
    return pl.pallas_call(
        lambda *refs: join_kernel(len(xs), *refs),
        in_specs=[pl.BlockSpec(memory_space=pl.ANY)] * len(xs),
        out_specs=[pl.BlockSpec(memory_space=pltpu.VMEM)] * parts,
        out_shape=[jax.ShapeDtypeStruct((rows, xs[0].shape[1]), xs[0].dtype)] * parts,
        scratch_shapes=[pltpu.SemaphoreType.DMA((len(xs),))],
        compiler_params=pltpu.CompilerParams(vmem_limit_bytes=12 * MIB),
        cost_estimate=SMALL,
        name="join_rows",
    )(*xs)


def after(value, *others):
    return lax.optimization_barrier((value, *others))[0]


def stats_kernel(n, *refs):
    xs, (gate_ref, up_ref, hid_in, feat_in, hid_ref, feat_ref, g_acc, u_acc) = refs[:n], refs[n:]
    f = lax.axis_index("ffn")

    def rows_of(cols):
        parts = [x_ref[:, cols] for x_ref in xs]
        return parts[0] if n == 1 else jnp.concatenate(parts, axis=0)

    x = rows_of(slice(0, STEP))
    x = jnp.where(x > LIMIT, jnp.zeros_like(x), x)
    g_acc[...] = jnp.dot(x, gate_ref[:STEP, :], preferred_element_type=jnp.float32)
    u_acc[...] = jnp.dot(x, up_ref[:STEP, :], preferred_element_type=jnp.float32)

    def step(k, carry):
        cols = pl.ds(pl.multiple_of(k * STEP, STEP), STEP)
        x = rows_of(cols)
        g_acc[...] += jnp.dot(x, gate_ref[cols, :], preferred_element_type=jnp.float32)
        u_acc[...] += jnp.dot(x, up_ref[cols, :], preferred_element_type=jnp.float32)
        return carry

    lax.fori_loop(1, gate_ref.shape[0] // STEP, step, 0)
    live = jnp.where(rows_of(slice(0, 128)).astype(jnp.float32) > LIMIT, 0.0, 1.0)
    feat_ref[:, 384:] = feat_in[:, 384:] + jnp.sum(live, axis=0, keepdims=True)
    part = rows_of(pl.ds(pl.multiple_of(f * 384, 128), 384)).astype(jnp.float32)
    part = jnp.where(part > LIMIT, 0.0, part)
    feat_ref[:, :384] = feat_in[:, :384] + jnp.sum(part * part, axis=0, keepdims=True)
    g = g_acc[...]
    h = g / (1.0 + jnp.exp(-g)) * u_acc[...]
    hid_ref[...] = hid_in[...] + jnp.sum(h * h, axis=0, keepdims=True)


def add_stats(xs, gate, up, hid, feat):
    width, units = gate.shape
    rows = sum(x.shape[0] for x in xs)
    vmem = pl.BlockSpec(memory_space=pltpu.VMEM)
    return pl.pallas_call(
        lambda *refs: stats_kernel(len(xs), *refs),
        in_specs=[vmem] * (len(xs) + 4),
        out_specs=[vmem] * 2,
        out_shape=[
            jax.ShapeDtypeStruct(hid.shape, jnp.float32),
            jax.ShapeDtypeStruct(feat.shape, jnp.float32),
        ],
        scratch_shapes=[pltpu.VMEM((rows, units), jnp.float32)] * 2,
        cost_estimate=pl.CostEstimate(
            flops=4 * rows * width * units,
            transcendentals=rows * units,
            bytes_accessed=2 * width * rows,
        ),
        compiler_params=pltpu.CompilerParams(vmem_limit_bytes=16 * MIB),
        name="hidden_stats",
    )(*xs, gate, up, hid, feat)


def fill_scale(scale_ref, hid_ref, feat_ref):
    rms = jnp.sqrt(hid_ref[...] / feat_ref[:, 384:385])
    scale_ref[...] = jnp.broadcast_to(16.0 * rms, (128, rms.shape[1])).T


def keep_of(down, scale, inverse):
    wide = jnp.concatenate([scale] * (down.shape[1] // 128), axis=1)
    return jnp.clip(jnp.abs(down).astype(jnp.float32) * wide * inverse - 15.5, 0.0, 1.0)


def share_kernel(hid_ref, feat_ref, down_ref, thr_ref, share_ref, scale_ref):
    fill_scale(scale_ref, hid_ref, feat_ref)

    def block(j, carry):
        cols = pl.ds(pl.multiple_of(j * SHARE_COLS, SHARE_COLS), SHARE_COLS)
        inverse = 1.0 / thr_ref[:, cols]
        total = jnp.zeros((8, SHARE_COLS), jnp.float32)
        for u in range(0, down_ref.shape[0], 64):
            keep = keep_of(down_ref[u : u + 64, cols], scale_ref[u : u + 64, :], inverse)
            total += jnp.sum(keep.reshape(8, 8, SHARE_COLS), axis=0)
        share_ref[:, cols] = jnp.sum(total, axis=0, keepdims=True) * (1.0 / FF)
        return carry

    lax.fori_loop(0, down_ref.shape[1] // SHARE_COLS, block, 0)


def share_pass(hid, feat, down, thresholds):
    vmem = pl.BlockSpec(memory_space=pltpu.VMEM)
    return pl.pallas_call(
        share_kernel,
        in_specs=[vmem] * 4,
        out_specs=vmem,
        out_shape=jax.ShapeDtypeStruct((1, down.shape[1]), jnp.float32),
        scratch_shapes=[pltpu.VMEM((down.shape[0], 128), jnp.float32)],
        compiler_params=pltpu.CompilerParams(vmem_limit_bytes=8 * MIB),
        name="share_pass",
    )(hid, feat, down, thresholds)


def keep_kernel(
    hid_ref, feat_ref, down_ref, thr_ref, keep_ref, rms_ref, scale_ref, inverse_ref, got, made, sem
):
    units, width = down_ref.shape
    blocks = [pl.ds(j * KEEP_ROWS, KEEP_ROWS) for j in range(units // KEEP_ROWS)]
    loads = [
        pltpu.make_async_copy(down_ref.at[rows], got.at[rows], sem.at[0, j])
        for j, rows in enumerate(blocks)
    ]
    stores = [
        pltpu.make_async_copy(made.at[j % 2], keep_ref.at[rows], sem.at[1, j])
        for j, rows in enumerate(blocks)
    ]
    for load in loads:
        load.start()
    fill_scale(scale_ref, hid_ref, feat_ref)
    inverse_ref[...] = 1.0 / thr_ref[...]
    rms_ref[...] = jnp.sqrt(feat_ref[:, :384] / feat_ref[:, 384:385])
    for j, rows in enumerate(blocks):
        loads[j].wait()
        if j >= 2:
            stores[j - 2].wait()

        def block(i, carry, j=j, rows=rows):
            cols = pl.ds(pl.multiple_of(i * KEEP_COLS, KEEP_COLS), KEEP_COLS)
            keep = keep_of(got[rows, cols], scale_ref[rows, :], inverse_ref[:, cols])
            made[j % 2, :, cols] = keep.astype(made.dtype)
            return carry

        lax.fori_loop(0, width // KEEP_COLS, block, 0)
        stores[j].start()
    stores[-2].wait()
    stores[-1].wait()


def keep_pass(hid, feat, down, thresholds):
    units, width = down.shape
    vmem = pl.BlockSpec(memory_space=pltpu.VMEM)
    return pl.pallas_call(
        keep_kernel,
        in_specs=[vmem, vmem, pl.BlockSpec(memory_space=pltpu.HBM), vmem],
        out_specs=[pl.BlockSpec(memory_space=pltpu.HBM), vmem],
        out_shape=[
            jax.ShapeDtypeStruct((units, width), down.dtype),
            jax.ShapeDtypeStruct((1, 384), jnp.float32),
        ],
        scratch_shapes=[
            pltpu.VMEM((units, 128), jnp.float32),
            pltpu.VMEM((1, width), jnp.float32),
            pltpu.VMEM((units, width), down.dtype),
            pltpu.VMEM((2, KEEP_ROWS, width), down.dtype),
            pltpu.SemaphoreType.DMA((2, units // KEEP_ROWS)),
        ],
        compiler_params=pltpu.CompilerParams(vmem_limit_bytes=12 * MIB),
        name="keep_pass",
    )(hid, feat, pltpu.with_memory_space_constraint(down, pltpu.HBM), thresholds)


def per_device(tokens, expert_ids, gate_weight, up_weight, down_weight, thresholds):
    gate, up, down = gate_weight[0], up_weight[0], down_weight[0]
    near, far = pack(tokens, expert_ids)
    own = for_this_core(near)
    far = for_this_core(after(far, own))
    far = over_z(far[24:48], 2), over_z(far[:24], 1), over_z(far[48:], -1)
    left, right = first_way(own, 1), first_way(own, -1)
    corner = first_way(left[:16], 1), first_way(right[16:], -1)
    [own_line] = joined([own, left, right, *corner], 1)

    *sides, own_line = lax.optimization_barrier((far[1], far[2], own_line))
    near_sides = second_way(own_line, 1), second_way(own_line, -1)
    [rest] = joined([far[0], *sides], 1)
    left, right = [first_way(rest[:40], 1)], [first_way(rest[40:], -1)]
    corner = first_way(left[0], 1), first_way(right[0], -1)
    left.append(first_way(rest[40:], 1))
    right.insert(0, first_way(rest[:40], -1))
    near_corner = second_way(near_sides[0][:48], 1), second_way(near_sides[1][48:], -1)

    [head] = joined([rest, *left], 1)
    corner, near_corner = lax.optimization_barrier((corner, near_corner))
    [tail] = joined([*right, *corner], 1)
    left, right = second_way(head, 1), second_way(tail, -1)
    left_too, right_too = second_way(tail, 1), second_way(head, -1)

    hid = jnp.zeros((1, 512), jnp.float32)
    feat = jnp.zeros((1, 512), jnp.float32)
    hid, feat = add_stats([own_line, *near_sides, *near_corner], gate, up, hid, feat)
    far_corner = second_way(left[:96], 1), second_way(right[:96], -1)
    hid, feat = add_stats([head, tail], gate, up, hid, feat)
    hid, feat = add_stats([left, right], gate, up, hid, feat)
    left, right, hid, feat = lax.optimization_barrier((left, right, hid, feat))
    last_corner = second_way(left[96:], 1), second_way(right[96:], -1)
    hid, feat = add_stats([left_too, right_too], gate, up, hid, feat)
    hid, feat = add_stats(list(far_corner), gate, up, hid, feat)
    hid, feat = add_stats(list(last_corner), gate, up, hid, feat)
    share = share_pass(hid, feat, down, thresholds)
    pieces = lax.all_to_all(share.reshape(16, 1, 384), "ffn", 0, 0, tiled=True)
    keep, input_rms = keep_pass(hid, feat, down, thresholds)
    return keep[None], jnp.sum(pieces, axis=0), input_rms


def solution(mesh):
    in_specs = (
        P(("expert", "ffn"), None),
        P(("expert", "ffn"), None),
        P("expert", None, "ffn"),
        P("expert", None, "ffn"),
        P("expert", "ffn", None),
        P("expert", None),
    )
    out_specs = (P("expert", "ffn", None), P("expert", "ffn"), P("expert", "ffn"))
    return jax.shard_map(
        per_device, mesh=mesh, in_specs=in_specs, out_specs=out_specs, check_vma=False
    )
```

```python
import jax
import jax.numpy as jnp
from jax import lax
from jax.experimental import pallas as pl
from jax.experimental.pallas import tpu as pltpu
from jax.sharding import PartitionSpec as P

FF = 8192
CAP = 12
MARK = 512.0
LIMIT = 100.0
RING = 4
AXES = ("expert", "ffn")
STEP = 768
KEEP_ROWS = 64
KEEP_COLS = 512
SHARE_COLS = 256
MIB = 1 << 20
SMALL = pl.CostEstimate(flops=0, transcendentals=0, bytes_accessed=0)


def moved(value, core0, core1):
    pairs = []
    for z in range(RING):
        for c in range(2):
            for y in range(RING):
                for x in range(RING):
                    dz, dc, dy, dx = core1 if c else core0
                    src = ((z * 2 + c) * RING + y) * RING + x
                    to = (((z + dz) % RING) * 2 + (c + dc) % 2) * RING + (y + dy) % RING
                    pairs.append((src, to * RING + (x + dx) % RING))
    return lax.ppermute(value, AXES, pairs)


def over_z(value, step):
    return moved(value, (step, 0, 0, 0), (step, 0, 0, 0))


def to_other_core(value):
    return moved(value, (0, 1, 0, 0), (0, 1, 0, 0))


def first_way(value, step):
    return moved(value, (0, 0, 0, step), (0, 0, step, 0))


def second_way(value, step):
    return moved(value, (0, 0, step, 0), (0, 0, 0, step))


def pack_kernel(ids_hbm, tokens_hbm, near_ref, far_ref, ids_ref, tokens_ref, sem):
    loads = (
        pltpu.make_async_copy(ids_hbm, ids_ref, sem.at[0]),
        pltpu.make_async_copy(tokens_hbm, tokens_ref, sem.at[1]),
    )
    for load in loads:
        load.start()
    loads[0].wait()
    expert = lax.axis_index("expert")
    z, c = expert // 2, expert % 2
    count = tokens_ref.shape[0]
    ids = ids_ref[...]
    before = lax.broadcasted_iota(jnp.int32, (count, count), 0) < lax.broadcasted_iota(
        jnp.int32, (count, count), 1
    )
    before = before.astype(jnp.float32).astype(jnp.bfloat16)

    def chosen(shifts):
        size = 2 * CAP * len(shifts)
        row = lax.broadcasted_iota(jnp.int32, (size, count), 0)
        group = row // CAP
        slot = row - group * CAP
        wanted = jnp.zeros((size, count), jnp.int32)
        for i, shift in enumerate(shifts):
            for j, core in enumerate((c, 1 - c)):
                chip = (z + shift) % RING
                wanted = jnp.where(group == 2 * i + j, chip * 2 + core, wanted)
        routed = (ids[0:1, :] == wanted) | (ids[1:2, :] == wanted)
        mark = routed.astype(jnp.float32)
        rank = jnp.dot(mark.astype(jnp.bfloat16), before, preferred_element_type=jnp.float32)
        pick = jnp.where(routed & (rank.astype(jnp.int32) == slot), 1.0, 0.0)
        filled = jnp.sum(pick, axis=1, keepdims=True)
        return pick.astype(jnp.bfloat16), filled

    def packed(out_ref, pick, filled):
        out = jnp.dot(pick, tokens_ref[...], preferred_element_type=jnp.float32)
        out_ref[...] = out.astype(jnp.bfloat16)
        head = out[:, :128]
        lane = lax.broadcasted_iota(jnp.int32, head.shape, 1)
        empty = (lane == 0) & (filled < 0.5)
        out_ref[:, :128] = jnp.where(empty, MARK, head).astype(jnp.bfloat16)

    near, far = chosen((0,)), chosen((1, 2, 3))
    loads[1].wait()
    packed(near_ref, *near)
    packed(far_ref, *far)


def pack(tokens, expert_ids):
    width = tokens.shape[1]
    ids = expert_ids.T
    return pl.pallas_call(
        pack_kernel,
        in_specs=[pl.BlockSpec(memory_space=pl.ANY)] * 2,
        scratch_shapes=[
            pltpu.VMEM(ids.shape, ids.dtype),
            pltpu.VMEM(tokens.shape, tokens.dtype),
            pltpu.SemaphoreType.DMA((2,)),
        ],
        out_shape=[jax.ShapeDtypeStruct((n * CAP, width), tokens.dtype) for n in (2, 6)],
        compiler_params=pltpu.CompilerParams(vmem_limit_bytes=12 * MIB),
        cost_estimate=SMALL,
        name="pack_rows",
    )(*(pltpu.with_memory_space_constraint(v, pltpu.HBM) for v in (ids, tokens)))


def for_this_core(value):
    row = lax.broadcasted_iota(jnp.int32, value.shape, 0)
    return jnp.where(row % (2 * CAP) < CAP, value, to_other_core(value))


def join_kernel(n, *refs):
    xs, outs, sem = refs[:n], refs[n:-1], refs[-1]
    copies, at = [], 0
    for i, x_ref in enumerate(xs):
        out_ref = outs[at // outs[0].shape[0]]
        rows = pl.ds(at % outs[0].shape[0], x_ref.shape[0])
        copies.append(pltpu.make_async_copy(x_ref, out_ref.at[rows], sem.at[i]))
        at += x_ref.shape[0]
    for copy in copies:
        copy.start()
    for copy in copies:
        copy.wait()


def joined(xs, parts):
    rows = sum(x.shape[0] for x in xs) // parts
    return pl.pallas_call(
        lambda *refs: join_kernel(len(xs), *refs),
        in_specs=[pl.BlockSpec(memory_space=pl.ANY)] * len(xs),
        out_specs=[pl.BlockSpec(memory_space=pltpu.VMEM)] * parts,
        out_shape=[jax.ShapeDtypeStruct((rows, xs[0].shape[1]), xs[0].dtype)] * parts,
        scratch_shapes=[pltpu.SemaphoreType.DMA((len(xs),))],
        compiler_params=pltpu.CompilerParams(vmem_limit_bytes=12 * MIB),
        cost_estimate=SMALL,
        name="join_rows",
    )(*xs)


def after(value, *others):
    return lax.optimization_barrier((value, *others))[0]


def stats_kernel(n, *refs):
    xs, (gate_ref, up_ref, hid_in, feat_in, hid_ref, feat_ref, g_acc, u_acc) = refs[:n], refs[n:]
    f = lax.axis_index("ffn")

    def rows_of(cols):
        parts = [x_ref[:, cols] for x_ref in xs]
        return parts[0] if n == 1 else jnp.concatenate(parts, axis=0)

    x = rows_of(slice(0, STEP))
    x = jnp.where(x > LIMIT, jnp.zeros_like(x), x)
    g_acc[...] = jnp.dot(x, gate_ref[:STEP, :], preferred_element_type=jnp.float32)
    u_acc[...] = jnp.dot(x, up_ref[:STEP, :], preferred_element_type=jnp.float32)

    def step(k, carry):
        cols = pl.ds(pl.multiple_of(k * STEP, STEP), STEP)
        x = rows_of(cols)
        g_acc[...] += jnp.dot(x, gate_ref[cols, :], preferred_element_type=jnp.float32)
        u_acc[...] += jnp.dot(x, up_ref[cols, :], preferred_element_type=jnp.float32)
        return carry

    lax.fori_loop(1, gate_ref.shape[0] // STEP, step, 0)
    live = jnp.where(rows_of(slice(0, 128)).astype(jnp.float32) > LIMIT, 0.0, 1.0)
    feat_ref[:, 384:] = feat_in[:, 384:] + jnp.sum(live, axis=0, keepdims=True)
    part = rows_of(pl.ds(pl.multiple_of(f * 384, 128), 384)).astype(jnp.float32)
    part = jnp.where(part > LIMIT, 0.0, part)
    feat_ref[:, :384] = feat_in[:, :384] + jnp.sum(part * part, axis=0, keepdims=True)
    g = g_acc[...]
    h = g / (1.0 + jnp.exp(-g)) * u_acc[...]
    hid_ref[...] = hid_in[...] + jnp.sum(h * h, axis=0, keepdims=True)


def add_stats(xs, gate, up, hid, feat):
    width, units = gate.shape
    rows = sum(x.shape[0] for x in xs)
    vmem = pl.BlockSpec(memory_space=pltpu.VMEM)
    return pl.pallas_call(
        lambda *refs: stats_kernel(len(xs), *refs),
        in_specs=[vmem] * (len(xs) + 4),
        out_specs=[vmem] * 2,
        out_shape=[
            jax.ShapeDtypeStruct(hid.shape, jnp.float32),
            jax.ShapeDtypeStruct(feat.shape, jnp.float32),
        ],
        scratch_shapes=[pltpu.VMEM((rows, units), jnp.float32)] * 2,
        cost_estimate=pl.CostEstimate(
            flops=4 * rows * width * units,
            transcendentals=rows * units,
            bytes_accessed=2 * width * rows,
        ),
        compiler_params=pltpu.CompilerParams(vmem_limit_bytes=16 * MIB),
        name="hidden_stats",
    )(*xs, gate, up, hid, feat)


def fill_scale(scale_ref, hid_ref, feat_ref):
    rms = jnp.sqrt(hid_ref[...] / feat_ref[:, 384:385])
    scale_ref[...] = jnp.broadcast_to(16.0 * rms, (128, rms.shape[1])).T


def keep_of(down, scale, inverse):
    wide = jnp.concatenate([scale] * (down.shape[1] // 128), axis=1)
    return jnp.clip(jnp.abs(down).astype(jnp.float32) * wide * inverse - 15.5, 0.0, 1.0)


def share_kernel(hid_ref, feat_ref, down_ref, thr_ref, share_ref, scale_ref):
    fill_scale(scale_ref, hid_ref, feat_ref)

    def block(j, carry):
        cols = pl.ds(pl.multiple_of(j * SHARE_COLS, SHARE_COLS), SHARE_COLS)
        inverse = 1.0 / thr_ref[:, cols]
        total = jnp.zeros((8, SHARE_COLS), jnp.float32)
        for u in range(0, down_ref.shape[0], 64):
            keep = keep_of(down_ref[u : u + 64, cols], scale_ref[u : u + 64, :], inverse)
            total += jnp.sum(keep.reshape(8, 8, SHARE_COLS), axis=0)
        share_ref[:, cols] = jnp.sum(total, axis=0, keepdims=True) * (1.0 / FF)
        return carry

    lax.fori_loop(0, down_ref.shape[1] // SHARE_COLS, block, 0)


def share_pass(hid, feat, down, thresholds):
    vmem = pl.BlockSpec(memory_space=pltpu.VMEM)
    return pl.pallas_call(
        share_kernel,
        in_specs=[vmem] * 4,
        out_specs=vmem,
        out_shape=jax.ShapeDtypeStruct((1, down.shape[1]), jnp.float32),
        scratch_shapes=[pltpu.VMEM((down.shape[0], 128), jnp.float32)],
        compiler_params=pltpu.CompilerParams(vmem_limit_bytes=8 * MIB),
        name="share_pass",
    )(hid, feat, down, thresholds)


def keep_kernel(
    hid_ref, feat_ref, down_ref, thr_ref, keep_ref, rms_ref, scale_ref, inverse_ref, got, made, sem
):
    units, width = down_ref.shape
    blocks = [pl.ds(j * KEEP_ROWS, KEEP_ROWS) for j in range(units // KEEP_ROWS)]
    loads = [
        pltpu.make_async_copy(down_ref.at[rows], got.at[rows], sem.at[0, j])
        for j, rows in enumerate(blocks)
    ]
    stores = [
        pltpu.make_async_copy(made.at[j % 2], keep_ref.at[rows], sem.at[1, j])
        for j, rows in enumerate(blocks)
    ]
    for load in loads:
        load.start()
    fill_scale(scale_ref, hid_ref, feat_ref)
    inverse_ref[...] = 1.0 / thr_ref[...]
    rms_ref[...] = jnp.sqrt(feat_ref[:, :384] / feat_ref[:, 384:385])
    for j, rows in enumerate(blocks):
        loads[j].wait()
        if j >= 2:
            stores[j - 2].wait()

        def block(i, carry, j=j, rows=rows):
            cols = pl.ds(pl.multiple_of(i * KEEP_COLS, KEEP_COLS), KEEP_COLS)
            keep = keep_of(got[rows, cols], scale_ref[rows, :], inverse_ref[:, cols])
            made[j % 2, :, cols] = keep.astype(made.dtype)
            return carry

        lax.fori_loop(0, width // KEEP_COLS, block, 0)
        stores[j].start()
    stores[-2].wait()
    stores[-1].wait()


def keep_pass(hid, feat, down, thresholds):
    units, width = down.shape
    vmem = pl.BlockSpec(memory_space=pltpu.VMEM)
    return pl.pallas_call(
        keep_kernel,
        in_specs=[vmem, vmem, pl.BlockSpec(memory_space=pltpu.HBM), vmem],
        out_specs=[pl.BlockSpec(memory_space=pltpu.HBM), vmem],
        out_shape=[
            jax.ShapeDtypeStruct((units, width), down.dtype),
            jax.ShapeDtypeStruct((1, 384), jnp.float32),
        ],
        scratch_shapes=[
            pltpu.VMEM((units, 128), jnp.float32),
            pltpu.VMEM((1, width), jnp.float32),
            pltpu.VMEM((units, width), down.dtype),
            pltpu.VMEM((2, KEEP_ROWS, width), down.dtype),
            pltpu.SemaphoreType.DMA((2, units // KEEP_ROWS)),
        ],
        compiler_params=pltpu.CompilerParams(vmem_limit_bytes=12 * MIB),
        name="keep_pass",
    )(hid, feat, pltpu.with_memory_space_constraint(down, pltpu.HBM), thresholds)


def per_device(tokens, expert_ids, gate_weight, up_weight, down_weight, thresholds):
    gate, up, down = gate_weight[0], up_weight[0], down_weight[0]
    near, far = pack(tokens, expert_ids)
    own = for_this_core(near)
    far = for_this_core(after(far, own))
    far = over_z(far[24:48], 2), over_z(far[:24], 1), over_z(far[48:], -1)
    left, right = first_way(own, 1), first_way(own, -1)
    corner = first_way(left[:16], 1), first_way(right[16:], -1)
    [own_line] = joined([own, left, right, *corner], 1)

    *sides, own_line = lax.optimization_barrier((far[1], far[2], own_line))
    near_sides = second_way(own_line, 1), second_way(own_line, -1)
    [rest] = joined([far[0], *sides], 1)
    left, right = [first_way(rest[:40], 1)], [first_way(rest[40:], -1)]
    corner = first_way(left[0], 1), first_way(right[0], -1)
    left.append(first_way(rest[40:], 1))
    right.insert(0, first_way(rest[:40], -1))
    near_corner = second_way(near_sides[0][:48], 1), second_way(near_sides[1][48:], -1)

    [head] = joined([rest, *left], 1)
    corner, near_corner = lax.optimization_barrier((corner, near_corner))
    [tail] = joined([*right, *corner], 1)
    left, right = second_way(head, 1), second_way(tail, -1)
    left_too, right_too = second_way(tail, 1), second_way(head, -1)

    hid = jnp.zeros((1, 512), jnp.float32)
    feat = jnp.zeros((1, 512), jnp.float32)
    hid, feat = add_stats([own_line, *near_sides, *near_corner], gate, up, hid, feat)
    far_corner = second_way(left[:96], 1), second_way(right[:96], -1)
    hid, feat = add_stats([head, tail], gate, up, hid, feat)
    hid, feat = add_stats([left, right], gate, up, hid, feat)
    left, right, hid, feat = lax.optimization_barrier((left, right, hid, feat))
    last_corner = second_way(left[96:], 1), second_way(right[96:], -1)
    hid, feat = add_stats([left_too, right_too], gate, up, hid, feat)
    hid, feat = add_stats(list(far_corner), gate, up, hid, feat)
    hid, feat = add_stats(list(last_corner), gate, up, hid, feat)
    share = share_pass(hid, feat, down, thresholds)
    pieces = lax.all_to_all(share.reshape(16, 1, 384), "ffn", 0, 0, tiled=True)
    keep, input_rms = keep_pass(hid, feat, down, thresholds)
    return keep[None], jnp.sum(pieces, axis=0), input_rms


def solution(mesh):
    in_specs = (
        P(("expert", "ffn"), None),
        P(("expert", "ffn"), None),
        P("expert", None, "ffn"),
        P("expert", None, "ffn"),
        P("expert", "ffn", None),
        P("expert", None),
    )
    out_specs = (P("expert", "ffn", None), P("expert", "ffn"), P("expert", "ffn"))
    return jax.shard_map(
        per_device, mesh=mesh, in_specs=in_specs, out_specs=out_specs, check_vma=False
    )
```
